256 devices in a mesh: ctx: 16 (over x, y_hi, core), tp: 16 (over z, y_lo).
Axes of the slice: x: 4, y: 4 (y_hi: 2, y_lo: 2; y = y_hi * 2 + y_lo), z: 8, core: 2. Of those that a mesh axis runs over, the one named last changes fastest.
Arguments:
- hidden: bfloat16 [4096, 8192], P('ctx', 'tp'), may hold values from -6 to 6
- w_feature: bfloat16 [8192, 3, 8192], P('ctx', None, 'tp'), may hold values from -0.0625 to 0.0625
- short_filter: float32 [7, 3, 8192], P(None, None, 'tp'), may hold values from -2.4 to 2.4
- mr_filter: bfloat16 [512, 128], P('tp'), may hold values from -0.5 to 0.5
- w_out: bfloat16 [8192, 8192], P('tp'), may hold values from -0.09375 to 0.09375
Outputs:
- mixed: bfloat16 [4096, 8192], P('ctx', 'tp')
The draws below stay inside these ranges and needn't reach their ends.
All inputs are finite; a program needn't handle non-finite values.
Results may differ from the reference program's by a relative error of at most 0.024.
Values may be sent and summed in bfloat16 or wider, within the bound.
No kernel may reach another device: no remote copies, remote signals or barrier semaphores. Data moves between devices by JAX's collectives and lax.ppermute only.
A program may use at most 128 MiB of HBM per device.

```python
import jax
import jax.numpy as jnp
from jax import lax

D = 8192
TAPS_SHORT = 7
TAPS_MR = 128
GROUP = 16
SEQ = 4096
N_CTX = 16


def spiked(entries, key, source, target, shards_of, factor):
    owner, partner = [(jnp.arange(entries.shape[position]) // (entries.shape[position] // shards_of)).reshape([-1 if axis == position else 1 for axis in range(entries.ndim)]) for position in (source, target)]
    chosen = jax.random.permutation(key, shards_of)[partner]
    strong = (owner == chosen) | (owner == (partner + shards_of // 2) % shards_of)
    return jnp.where(strong, factor * entries, entries)


def level_of(stream_key, extent, pieces, least, high):
    loudness = 1.0
    for axis_at, blocks in pieces:
        steps = jax.random.uniform(jax.random.fold_in(jax.random.fold_in(stream_key, 6), axis_at), (blocks,), jnp.float32, least / len(pieces), high / len(pieces))
        loudness = loudness * jnp.repeat(jnp.exp(steps), extent[axis_at] // blocks).reshape((-1,) + (1,) * (len(extent) - 1 - axis_at))
    return loudness


def gaussian(stream_key, shape, deviation, most, pieces=(), kind=jnp.bfloat16):
    level = level_of(stream_key, shape, pieces, -0.22, 0.18) if pieces else 1.0
    array = jax.random.normal(stream_key, shape, jnp.float32) * deviation * level
    return jnp.minimum(jnp.maximum(array, -most), most).astype(kind)


def bell_draw_with(own_key, dims, scale, most, split, heavy, held_as=jnp.bfloat16):
    array = scale * jax.random.normal(own_key, dims, jnp.float32)
    if split:
        array = array * level_of(own_key, dims, split, -0.22, 0.18)
    return jnp.clip(spiked(array, jax.random.fold_in(own_key, 3), *heavy), -most, most).astype(held_as)


def setup_inputs(seed: int = 0) -> dict:
    key_list = jax.random.split(jax.random.key(seed), 6)
    hidden = bell_draw_with(key_list[0], (SEQ, D), 1.0, 6.0, ((0, 16), (1, 16)), (1, 0, 16, 2.0))
    w_feature = gaussian(key_list[1], (D, 3, D), D ** -0.5, 0.0625, ((0, 16), (2, 16)))
    short_filter = gaussian(key_list[2], (TAPS_SHORT, 3, D), 0.4, 2.4, ((2, 16),), jnp.float32)
    mr_filter = gaussian(key_list[3], (D // GROUP, TAPS_MR), TAPS_MR ** -0.5, 0.5, ((0, 16),))
    w_out = bell_draw_with(key_list[4], (D, D), D ** -0.5, 0.09375, ((0, 16),), (0, 1, 16, 2.0))
    return dict(hidden=hidden, w_feature=w_feature, short_filter=short_filter, mr_filter=mr_filter, w_out=w_out)


def short_filtering(padded, tap_weights, row_count):
    running = jnp.zeros((row_count,) + padded.shape[1:], jnp.float32)
    for shift_by in range(TAPS_SHORT):
        row_start = TAPS_SHORT - 1 - shift_by
        running = running + tap_weights[shift_by] * padded[row_start:row_start + row_count]
    return running


def reference(hidden, w_feature, short_filter, mr_filter, w_out):
    feature_block = D // N_CTX
    flat_weight = w_feature.reshape(D, 3 * D)

    def add_block(running, block_index):
        row_start = block_index * feature_block
        columns = lax.dynamic_slice_in_dim(hidden, row_start, feature_block, 1)
        weights = lax.dynamic_slice_in_dim(flat_weight, row_start, feature_block, 0)
        partial_sum = jnp.dot(columns, weights, preferred_element_type=jnp.float32).astype(jnp.bfloat16)
        partial_sum = lax.optimization_barrier(partial_sum)
        return running + partial_sum.astype(jnp.float32), None

    projected, unused = lax.scan(add_block, jnp.zeros((SEQ, 3 * D), jnp.float32),
                                 jnp.arange(N_CTX, dtype=jnp.int32))
    projected = projected.reshape(SEQ, 3, D)
    padded = jnp.pad(projected, ((TAPS_SHORT - 1, 0), (0, 0), (0, 0)))
    streams = short_filtering(padded, short_filter, SEQ)
    gated_rows = (streams[:, 1] * streams[:, 2]).astype(jnp.bfloat16)
    gated_rows = lax.optimization_barrier(gated_rows)
    channel_taps = jnp.repeat(mr_filter.astype(jnp.float32), GROUP, axis=0)
    gated_pad = jnp.pad(gated_rows.astype(jnp.float32), ((TAPS_MR - 1, 0), (0, 0)))

    def add_tap(running, tap_index):
        shifted = lax.dynamic_slice_in_dim(gated_pad, TAPS_MR - 1 - tap_index, SEQ, 0)
        weight_row = lax.dynamic_slice_in_dim(channel_taps, tap_index, 1, 1)[:, 0]
        return running + shifted * weight_row[None, :], None

    long_out, unused_taps = lax.scan(add_tap, jnp.zeros((SEQ, D), jnp.float32),
                                     jnp.arange(TAPS_MR, dtype=jnp.int32))
    mixer_rows = (streams[:, 0] * long_out).astype(jnp.bfloat16)
    return jnp.dot(mixer_rows, w_out, preferred_element_type=jnp.float32).astype(jnp.bfloat16)
```

```python
import jax
import jax.numpy as jnp
from jax import lax
from jax.sharding import PartitionSpec as P

TAPS_SHORT = 7
TAPS_MR = 128
GROUP = 16
NX, NZ = 4, 8


def pairs_of(move):
    out = []
    for x in range(NX):
        for yh in range(2):
            for core in range(2):
                for z in range(NZ):
                    for yl in range(2):
                        to = move(x, yh, core, z, yl)
                        if to is None:
                            continue
                        tx, tyh, tcore, tz, tyl = to
                        here = ((x * 2 + yh) * 2 + core) * 16 + z * 2 + yl
                        there = ((tx * 2 + tyh) * 2 + tcore) * 16 + tz * 2 + tyl
                        out.append((here, there))
    return out


def send(value, move):
    return lax.ppermute(value, ("ctx", "tp"), pairs_of(move))


def along_x(by):
    return lambda x, yh, core, z, yl: ((x + by) % NX, yh, core, z, yl)


def along_z(by):
    return lambda x, yh, core, z, yl: (x, yh, core, (z + by) % NZ, yl)


def other_yh(x, yh, core, z, yl):
    return x, 1 - yh, core, z, yl


def other_core(x, yh, core, z, yl):
    return x, yh, 1 - core, z, yl


def other_yl(x, yh, core, z, yl):
    return x, yh, core, z, 1 - yl


def swapped(x, yh, core, z, yl):
    return z // 2, yh, core, 2 * x + ((z % 2) ^ yh), yl ^ core


def next_block(x, yh, core, z, yl):
    block = (x * 2 + yh) * 2 + core + 1
    if block == 16:
        return None
    return block // 4, (block // 2) % 2, block % 2, z, yl


def short_filtering(extended, tap_weights):
    row_count = extended.shape[0] - (TAPS_SHORT - 1)
    running = jnp.zeros((row_count,) + extended.shape[1:], jnp.float32)
    for shift_by in range(TAPS_SHORT):
        row_start = TAPS_SHORT - 1 - shift_by
        running = running + tap_weights[shift_by] * extended[row_start : row_start + row_count]
    return running


def toeplitz_of(filters):
    shape = (TAPS_MR, 2 * TAPS_MR, TAPS_MR)
    out_pos = lax.broadcasted_iota(jnp.int32, shape, 0)
    in_pos = lax.broadcasted_iota(jnp.int32, shape, 1)
    tap_pos = lax.broadcasted_iota(jnp.int32, shape, 2)
    picker = (out_pos + (TAPS_MR - 1) - in_pos == tap_pos).astype(jnp.bfloat16)
    return jnp.einsum(
        "asj,gj->gas", picker, filters, preferred_element_type=jnp.float32
    ).astype(jnp.bfloat16)


def long_filtering(gated_ext, toeplitz, out_count):
    channel_count = gated_ext.shape[1]
    groups = toeplitz.shape[0]
    blocks = -(-out_count // TAPS_MR)
    pad_rows = (blocks + 1) * TAPS_MR - gated_ext.shape[0]
    padded = jnp.pad(gated_ext, ((0, pad_rows), (0, 0)))
    tile_rows = padded.reshape(blocks + 1, TAPS_MR, groups, GROUP)
    windows = jnp.concatenate([tile_rows[:-1], tile_rows[1:]], axis=1)
    result = jnp.einsum("gas,bsgc->bagc", toeplitz, windows, preferred_element_type=jnp.float32)
    return result.reshape(blocks * TAPS_MR, channel_count)


def dot(a, b):
    return jnp.dot(a, b, preferred_element_type=jnp.float32)


def local(hidden, w_feature, short_filter, mr_filter, w_out):
    rows, feats = hidden.shape
    slab = w_feature.shape[2]
    ctx = lax.axis_index("ctx")
    tp = lax.axis_index("tp")
    x = ctx // 4
    z, yl = tp // 2, tp % 2

    w_own = w_feature.reshape(feats, 3 * slab)
    w_yh = send(w_own, other_yh)
    w_core = send(w_own, other_core)
    w_both = send(w_yh, other_core)
    weights = jnp.concatenate([w_own, w_core, w_yh, w_both], 0)

    mine = send(hidden, swapped)
    beside = send(mine, other_yl)
    held = jnp.zeros((NX * rows, 4 * feats), jnp.bfloat16)

    def placed(held, block, by, other):
        zs = (z + by + NZ) % NZ
        row = ((zs // 2 - x + NX) % NX) * rows
        col = ((zs % 2) * 2 + (yl ^ other)) * feats
        return lax.dynamic_update_slice(held, block, (row, col))

    for other, block in ((0, mine), (1, beside)):
        held = placed(held, block, 0, other)
        up = down = block
        for step in range(1, 5):
            if step < 4 or other == 0:
                up = send(up, along_z(1))
                held = placed(held, up, -step, other)
            if step < 4 or other == 1:
                down = send(down, along_z(-1))
                held = placed(held, down, step, other)

    partial = dot(held, weights).astype(jnp.bfloat16)
    projected = partial[:rows].astype(jnp.float32)
    for by in (1, 2, 3):
        got = send(partial[by * rows : (by + 1) * rows], along_x(by))
        projected = projected + got.astype(jnp.float32)
    projected = projected.reshape(rows, 3, slab)

    rim = TAPS_SHORT - 1 + TAPS_MR - 1
    rim_rows = send(projected[rows - rim :, 1:].astype(jnp.bfloat16), next_block).astype(jnp.float32)
    q_rim = send(projected[rows - TAPS_SHORT + 1 :, 0].astype(jnp.bfloat16), next_block).astype(
        jnp.float32
    )
    queries = short_filtering(
        jnp.concatenate([q_rim, projected[:, 0]], 0), short_filter[:, 0]
    )
    pair = short_filtering(jnp.concatenate([rim_rows, projected[:, 1:]], 0), short_filter[:, 1:])
    gated_ext = (pair[:, 0] * pair[:, 1]).astype(jnp.bfloat16)
    long_out = long_filtering(gated_ext, toeplitz_of(mr_filter), rows)
    mixer = (queries * long_out).astype(jnp.bfloat16)

    width = w_out.shape[1] // NZ

    def part(by, lo, hi):
        start = ((z + by + NZ) % NZ) * width + lo
        return dot(mixer, lax.dynamic_slice_in_dim(w_out, start, hi - lo, 1))

    half = width // 2
    total = part(0, 0, width)
    up = part(4, 0, half).astype(jnp.bfloat16)
    down = part(-4, half, width).astype(jnp.bfloat16)
    ups, downs = [up, None], [None, down]
    for step in range(1, 5):
        ups = [None if u is None else send(u, along_z(1)) for u in ups]
        downs = [None if d is None else send(d, along_z(-1)) for d in downs]
        for h in (0, 1):
            lo = h * half
            mine_up = part(4 - step, lo, lo + half) if step < 4 else total[:, lo : lo + half]
            mine_down = part(step - 4, lo, lo + half) if step < 4 else None
            if step < 4:
                u, d = ups[h], downs[h]
                ups[h] = (mine_up if u is None else mine_up + u.astype(jnp.float32)).astype(jnp.bfloat16)
                downs[h] = (mine_down if d is None else mine_down + d.astype(jnp.float32)).astype(jnp.bfloat16)
    sums = [
        total[:, h * half : (h + 1) * half]
        + ups[h].astype(jnp.float32)
        + downs[h].astype(jnp.float32)
        for h in (0, 1)
    ]
    first = yl == 0
    away = jnp.where(first, sums[1], sums[0]).astype(jnp.bfloat16)
    stays = jnp.where(first, sums[0], sums[1])
    return (stays + send(away, other_yl).astype(jnp.float32)).astype(jnp.bfloat16)


def solution(mesh):
    return jax.shard_map(
        local,
        mesh=mesh,
        in_specs=(
            P("ctx", "tp"),
            P("ctx", None, "tp"),
            P(None, None, "tp"),
            P("tp", None),
            P("tp", None),
        ),
        out_specs=P("ctx", "tp"),
        check_vma=False,
    )
```

```python
import jax
import jax.numpy as jnp
from jax import lax
from jax.experimental import pallas as pl
from jax.experimental.pallas import tpu as pltpu
from jax.sharding import PartitionSpec as P

TAPS_SHORT = 7
TAPS_MR = 128
GROUP = 16
NX, NZ = 4, 8
RIM = 136
TILE = 256


def pairs_of(move):
    out = []
    for x in range(NX):
        for yh in range(2):
            for core in range(2):
                for z in range(NZ):
                    for yl in range(2):
                        to = move(x, yh, core, z, yl)
                        if to is None:
                            continue
                        tx, tyh, tcore, tz, tyl = to
                        here = ((x * 2 + yh) * 2 + core) * 16 + z * 2 + yl
                        there = ((tx * 2 + tyh) * 2 + tcore) * 16 + tz * 2 + tyl
                        out.append((here, there))
    return out


def send(value, move):
    return lax.ppermute(value, ("ctx", "tp"), pairs_of(move))


def along_z(by):
    return lambda x, yh, core, z, yl: (x, yh, core, (z + by) % NZ, yl)


def other_yh(x, yh, core, z, yl):
    return x, 1 - yh, core, z, yl


def other_core(x, yh, core, z, yl):
    return x, yh, 1 - core, z, yl


def other_yl(x, yh, core, z, yl):
    return x, yh, core, z, 1 - yl


def swapped(x, yh, core, z, yl):
    return z // 2, yh, core, 2 * ((x - z // 2) % NX) + z % 2, yl


def to_partner(x, yh, core, z, yl):
    return x, yh, core, z ^ 1, yl


def to_other(x, yh, core, z, yl):
    return x, yh, core, (z + (1 if z % 2 else -1)) % NZ, yl


def to_tokens(even, odd):
    return lambda x, yh, core, z, yl: ((x + z // 2 + (odd if z % 2 else even)) % NX, yh, core, z, yl)


def next_block(x, yh, core, z, yl):
    block = (x * 2 + yh) * 2 + core + 1
    if block == 16:
        return None
    return block // 4, (block // 2) % 2, block % 2, z, yl


def product_kernel(order_ref, a_ref, b_ref, c_ref, d_ref, w0_ref, w1_ref, w2_ref, w3_ref, out_ref, held):
    @pl.when(pl.program_id(0) == 0)
    def _():
        for slot, ref in enumerate((a_ref, b_ref, c_ref, d_ref)):
            held[order_ref[slot]] = ref[...]

    total = None
    for part, w_ref in enumerate((w0_ref, w1_ref, w2_ref, w3_ref)):
        term = jnp.dot(held[part], w_ref[0], preferred_element_type=jnp.float32)
        total = term if total is None else total + term
    out_ref[...] = total.astype(jnp.bfloat16)


def product(order, blocks, weights):
    rows, feats = blocks[0].shape
    slab = weights[0].shape[2]
    per = slab // TILE
    block = pl.BlockSpec((rows, feats), lambda j: (0, 0))
    tile = pl.BlockSpec((1, feats, TILE), lambda j: (j // per, 0, j % per))
    return pl.pallas_call(
        product_kernel,
        grid=(3 * per,),
        out_shape=jax.ShapeDtypeStruct((rows, 3 * slab), jnp.bfloat16),
        in_specs=[pl.BlockSpec(memory_space=pltpu.SMEM)] + [block] * 4 + [tile] * 4,
        out_specs=pl.BlockSpec((rows, TILE), lambda j: (0, j)),
        scratch_shapes=[pltpu.VMEM((4, rows, feats), jnp.bfloat16)],
        name="product",
    )(order, *blocks, *weights)


def spread_kernel(index_ref, own_ref, other_ref, w_ref, g_ref, out_ref):
    out_ref[0] = jnp.dot(own_ref[...], w_ref[...], preferred_element_type=jnp.float32) + jnp.dot(
        other_ref[...], g_ref[0], preferred_element_type=jnp.float32
    )


def spread(index, own, other, w_own, w_other):
    rows, depth = own.shape
    width = w_other.shape[2]
    count = index.shape[1]
    whole = pl.BlockSpec((rows, depth), lambda i, at: (0, 0))
    return pl.pallas_call(
        spread_kernel,
        out_shape=jax.ShapeDtypeStruct((count, rows, width), jnp.float32),
        grid_spec=pltpu.PrefetchScalarGridSpec(
            num_scalar_prefetch=1,
            grid=(count,),
            in_specs=[
                whole,
                whole,
                pl.BlockSpec((depth, width), lambda i, at: (0, at[0, i])),
                pl.BlockSpec((1, depth, width), lambda i, at: (at[1, i], 0, 0)),
            ],
            out_specs=pl.BlockSpec((1, rows, width), lambda i, at: (i, 0, 0)),
        ),
        name="spread",
    )(index, own, other, w_own, w_other)


def toeplitz_kernel(taps_ref, out_ref):
    for group in range(out_ref.shape[0]):
        row = jnp.broadcast_to(taps_ref[group : group + 1, :], (TAPS_MR, 2 * TAPS_MR))
        out_ref[group] = pltpu.roll(row, 0, 1, stride=1, stride_axis=0).astype(jnp.bfloat16)


def toeplitz_of(filters):
    groups = filters.shape[0]
    taps = jnp.pad(filters[:, ::-1].astype(jnp.float32), ((0, 0), (1, TAPS_MR - 1)))
    return pl.pallas_call(
        toeplitz_kernel,
        out_shape=jax.ShapeDtypeStruct((groups, TAPS_MR, 2 * TAPS_MR), jnp.bfloat16),
        in_specs=[pl.BlockSpec(memory_space=pltpu.VMEM)],
        out_specs=pl.BlockSpec(memory_space=pltpu.VMEM),
        name="toeplitz",
    )(taps)


def filter_kernel(proj_ref, rim_ref, qrim_ref, taps_ref, toep_ref, out_ref, k_ref, v_ref, q_ref, g_ref):
    rows, slab = out_ref.shape
    lane = lax.broadcasted_iota(jnp.int32, (2 * TAPS_MR, TILE), 1) // GROUP

    def filtered(ref, first, count, stream, start):
        total = None
        for by in range(TAPS_SHORT):
            tap = taps_ref[stream, pl.ds(by, 1), pl.ds(start, TILE)]
            term = tap * ref[pl.ds(first - by, count), :]
            total = term if total is None else total + term
        return total

    for start in range(0, slab, TILE):
        k_ref[pl.ds(0, RIM), :] = rim_ref[:, pl.ds(start, TILE)].astype(jnp.float32)
        v_ref[pl.ds(0, RIM), :] = rim_ref[:, pl.ds(slab + start, TILE)].astype(jnp.float32)
        q_ref[pl.ds(0, 8), :] = qrim_ref[pl.ds(8, 8), pl.ds(start, TILE)].astype(jnp.float32)
        k_ref[pl.ds(RIM, rows), :] = proj_ref[:, pl.ds(slab + start, TILE)]
        v_ref[pl.ds(RIM, rows), :] = proj_ref[:, pl.ds(2 * slab + start, TILE)]
        q_ref[pl.ds(8, rows), :] = proj_ref[:, pl.ds(start, TILE)]
        for block in range((rows + TAPS_MR) // TAPS_MR):
            first = block * TAPS_MR + RIM - TAPS_MR
            gate = filtered(k_ref, first, TAPS_MR, 1, start) * filtered(v_ref, first, TAPS_MR, 2, start)
            g_ref[pl.ds(block * TAPS_MR, TAPS_MR), :] = gate.astype(jnp.bfloat16)
        for block in range(rows // TAPS_MR):
            window = g_ref[pl.ds(block * TAPS_MR, 2 * TAPS_MR), :]
            total = None
            for group in range(TILE // GROUP):
                picked = jnp.where(lane == group, window, jnp.zeros_like(window))
                term = jnp.dot(
                    toep_ref[start // GROUP + group], picked, preferred_element_type=jnp.float32
                )
                total = term if total is None else total + term
            query = filtered(q_ref, 8 + block * TAPS_MR, TAPS_MR, 0, start)
            out_ref[pl.ds(block * TAPS_MR, TAPS_MR), pl.ds(start, TILE)] = (query * total).astype(jnp.bfloat16)


def filtering(projected, rim, qrim, taps, toeplitz):
    rows = projected.shape[0]
    slab = projected.shape[1] // 3
    whole = pl.BlockSpec(memory_space=pltpu.VMEM)
    return pl.pallas_call(
        filter_kernel,
        out_shape=jax.ShapeDtypeStruct((rows, slab), jnp.bfloat16),
        in_specs=[whole] * 5,
        out_specs=whole,
        scratch_shapes=[
            pltpu.VMEM((RIM + rows, TILE), jnp.float32),
            pltpu.VMEM((RIM + rows, TILE), jnp.float32),
            pltpu.VMEM((8 + rows, TILE), jnp.float32),
            pltpu.VMEM((TAPS_MR + rows, TILE), jnp.bfloat16),
        ],
        name="filters",
    )(projected, rim, qrim, taps, toeplitz)


def local(hidden, w_feature, short_filter, mr_filter, w_out):
    rows, _ = hidden.shape
    slab = w_feature.shape[2]
    ctx, tp = lax.axis_index("ctx"), lax.axis_index("tp")
    z, yl = tp // 2, tp % 2
    yh, core = (ctx // 2) % 2, ctx % 2
    order = jnp.stack([((z % 2) ^ yh ^ s) * 2 + (yl ^ core ^ e) for s in (0, 1) for e in (0, 1)])
    order = order.astype(jnp.int32)

    toeplitz = toeplitz_of(mr_filter)
    w_own = w_feature.transpose(1, 0, 2)
    mine = send(hidden, swapped)
    w_yh = send(w_own, other_yh)
    w_core = send(w_own, other_core)
    mine, toeplitz = lax.optimization_barrier((mine, toeplitz))
    own = [mine, send(mine, other_yl)]
    t1, o1, t2, o2, t3, o3, last = [], [], [], [], [], [], []
    for e in (0, 1):
        t1.append(send(own[e], to_partner))
        o1.append(send(own[e], to_other))
        t2.append(send(o1[e], to_partner))
        o2.append(send(t1[e], to_other))
        t3.append(send(o2[e], to_partner))
        o3.append(send(t2[e], to_other))
        last.append(send(t3[1], to_other) if e else send(o3[0], to_partner))
    w_both = send(w_yh, other_core)

    width = w_out.shape[1] // (2 * NZ)
    away = jnp.stack(
        [
            lax.dynamic_slice_in_dim(w_out, ((core * 4 + t) * 2 + 1 - yl) * width, width, 1)
            for t in range(4)
        ]
    )
    w_near = send(away, other_yl)
    w_far = send(w_near, other_core)
    w_other = jnp.concatenate([w_near, w_far], 0)

    weights = (w_own, w_core, w_yh, w_both)
    token_blocks = (
        (own, t1, (0, 0)),
        (o2, o1, (-1, 1)),
        (t2, t3, (1, -1)),
        (last, o3, (2, 2)),
    )
    projected = jnp.zeros((rows, 3 * slab), jnp.float32)
    for same, across, (even, odd) in token_blocks:
        partial = product(order, (*same, *across), weights)
        sent = send(partial, to_tokens(even, odd))
        projected = projected + sent.astype(jnp.float32)

    rim = send(projected[rows - RIM :, slab:].astype(jnp.bfloat16), next_block)
    qrim = send(projected[rows - 16 :, :slab].astype(jnp.bfloat16), next_block)
    mixer = filtering(projected, rim, qrim, short_filter.transpose(1, 0, 2), toeplitz)
    mixer_other = send(mixer, other_yl)

    shifts = (4, 3, -3, 2, -2, 1, -1, 0)
    to = jnp.stack([(z + by + NZ) % NZ for by in shifts])
    index = jnp.stack([to * 2 + yl, ((to // 4) ^ core) * 4 + to % 4]).astype(jnp.int32)
    early = spread(index[:, :3], mixer, mixer_other, w_out, w_other)
    later, early = lax.optimization_barrier((index[:, 3:], early))
    late = spread(later, mixer, mixer_other, w_out, w_other)
    part = {by: early[i] if i < 3 else late[i - 3] for i, by in enumerate(shifts)}
    half = width // 2
    cols = [slice(0, half), slice(half, width)]
    ups = [part[4][:, cols[0]].astype(jnp.bfloat16), None]
    downs = [None, part[4][:, cols[1]].astype(jnp.bfloat16)]
    for step in range(1, 5):
        ups = [None if u is None else send(u, along_z(1)) for u in ups]
        downs = [None if d is None else send(d, along_z(-1)) for d in downs]
        if step == 4:
            break
        for h in (0, 1):
            up, down = part[4 - step][:, cols[h]], part[step - 4][:, cols[h]]
            if ups[h] is not None:
                up = up + ups[h].astype(jnp.float32)
            if downs[h] is not None:
                down = down + downs[h].astype(jnp.float32)
            ups[h], downs[h] = up.astype(jnp.bfloat16), down.astype(jnp.bfloat16)
    sums = [
        part[0][:, cols[h]] + ups[h].astype(jnp.float32) + downs[h].astype(jnp.float32) for h in (0, 1)
    ]
    return jnp.concatenate(sums, 1).astype(jnp.bfloat16)


def solution(mesh):
    return jax.shard_map(
        local,
        mesh=mesh,
        in_specs=(
            P("ctx", "tp"),
            P("ctx", None, "tp"),
            P(None, None, "tp"),
            P("tp", None),
            P("tp", None),
        ),
        out_specs=P("ctx", "tp"),
        check_vma=False,
    )
```

```python
import functools

import jax
import jax.numpy as jnp
from jax import lax
from jax.experimental import pallas as pl
from jax.experimental.pallas import tpu as pltpu
from jax.sharding import PartitionSpec as P

TAPS_SHORT = 7
TAPS_MR = 128
GROUP = 16
NX, NZ = 4, 8
RIM = 136
TILE = 256


def pairs_of(move):
    out = []
    for x in range(NX):
        for yh in range(2):
            for core in range(2):
                for z in range(NZ):
                    for yl in range(2):
                        to = move(x, yh, core, z, yl)
                        if to is None:
                            continue
                        tx, tyh, tcore, tz, tyl = to
                        here = ((x * 2 + yh) * 2 + core) * 16 + z * 2 + yl
                        there = ((tx * 2 + tyh) * 2 + tcore) * 16 + tz * 2 + tyl
                        out.append((here, there))
    return out


def send(value, move):
    return lax.ppermute(value, ("ctx", "tp"), pairs_of(move))


def along_x(by):
    return lambda x, yh, core, z, yl: ((x + by) % NX, yh, core, z, yl)


def along_z(by):
    return lambda x, yh, core, z, yl: (x, yh, core, (z + by) % NZ, yl)


def other_yh(x, yh, core, z, yl):
    return x, 1 - yh, core, z, yl


def other_core(x, yh, core, z, yl):
    return x, yh, 1 - core, z, yl


def other_yl(x, yh, core, z, yl):
    return x, yh, core, z, 1 - yl


def swapped(x, yh, core, z, yl):
    return x, z % 2, yl, z - z % 2 + yh, core


def to_partner(x, yh, core, z, yl):
    return x, yh, core, z ^ 1, yl


def to_other(x, yh, core, z, yl):
    return x, yh, core, (z + (1 if z % 2 else -1)) % NZ, yl


def next_block(x, yh, core, z, yl):
    block = (x * 2 + yh) * 2 + core + 1
    if block == 16:
        return None
    return block // 4, (block // 2) % 2, block % 2, z, yl


def in_vmem(value):
    return pltpu.with_memory_space_constraint(value, pltpu.VMEM)


def kernel_of(body, out, scalars=0, scratch=()):
    whole = pl.BlockSpec(memory_space=pltpu.VMEM)

    def call(*args):
        placed = [*args[:scalars], *(in_vmem(a) for a in args[scalars:])]
        return pl.pallas_call(
            body,
            out_shape=pltpu.VMEM(*out),
            in_specs=[pl.BlockSpec(memory_space=pltpu.SMEM)] * scalars + [whole] * (len(args) - scalars),
            out_specs=whole,
            scratch_shapes=list(scratch),
            compiler_params=pltpu.CompilerParams(vmem_limit_bytes=16 << 20),
        )(*placed)

    return call


def arrange_kernel(order_ref, *refs):
    out_ref = refs[-1]
    for slot, ref in enumerate(refs[:-1]):
        out_ref[order_ref[slot]] = ref[...]


def product_kernel(stream, held_ref, *refs):
    out_ref = refs[-1]
    rows = held_ref.shape[1]

    @pl.loop(0, 2 * (out_ref.shape[2] // TILE))
    def _(at_tile):
        cols = pl.ds(pl.multiple_of((at_tile // 2) * TILE, TILE), TILE)
        first = (at_tile % 2) * 2
        total = None
        for part, ref, at, lo, count in stream(refs[:-1]):
            left = held_ref[pl.ds(part * 4 + first, 2), :, pl.ds(lo, count)].reshape(2 * rows, count)
            right = ref[:, cols] if at is None else ref[at, :, cols]
            term = jnp.dot(left, right, preferred_element_type=jnp.float32)
            total = term if total is None else total + term
        out_ref[pl.ds(first, 2), :, cols] = total.astype(jnp.bfloat16).reshape(2, rows, TILE)


def columns_kernel(at_ref, w_ref, out_ref, sems):
    width = out_ref.shape[2]
    copies = []
    for i in range(out_ref.shape[0]):
        cols = pl.ds(pl.multiple_of(at_ref[i] * width, width), width)
        copies.append(pltpu.make_async_copy(w_ref.at[:, cols], out_ref.at[i], sems.at[i]))
        copies[-1].start()
    for copy in copies:
        copy.wait()


def columns_of(at, w, width):
    count = at.shape[0]
    return pl.pallas_call(
        columns_kernel,
        out_shape=pltpu.VMEM((count, w.shape[0], width), w.dtype),
        in_specs=[pl.BlockSpec(memory_space=pltpu.SMEM), pl.BlockSpec(memory_space=pltpu.HBM)],
        out_specs=pl.BlockSpec(memory_space=pltpu.VMEM),
        scratch_shapes=[pltpu.SemaphoreType.DMA((count,))],
        compiler_params=pltpu.CompilerParams(vmem_limit_bytes=16 << 20),
        name="columns",
    )(at.astype(jnp.int32), pltpu.with_memory_space_constraint(w, pltpu.HBM))


def spread_own_kernel(own_ref, w_ref, out_ref):
    @pl.loop(0, out_ref.shape[0])
    def _(i):
        out_ref[i] = jnp.dot(own_ref[...], w_ref[i], preferred_element_type=jnp.float32)


def spread_kernel(lo, index_ref, other_ref, near_ref, far_ref, base_ref, out_ref, held):
    @pl.loop(0, out_ref.shape[0])
    def _(i):
        to = index_ref[1, lo + i]

        @pl.when(index_ref[0, lo + i] == 0)
        def _():
            held[...] = near_ref[to]

        @pl.when(index_ref[0, lo + i] != 0)
        def _():
            held[...] = far_ref[to]

        out_ref[i] = base_ref[lo + i] + jnp.dot(
            other_ref[...], held[...], preferred_element_type=jnp.float32
        )


def toeplitz_kernel(taps_ref, out_ref):
    @pl.loop(0, out_ref.shape[0])
    def _(group):
        row = jnp.broadcast_to(taps_ref[pl.ds(group, 1), :], (TAPS_MR, 2 * TAPS_MR))
        out_ref[group] = pltpu.roll(row, 0, 1, stride=1, stride_axis=0).astype(jnp.bfloat16)


def toeplitz_of(filters):
    groups = filters.shape[0]
    taps = jnp.pad(filters[:, ::-1].astype(jnp.float32), ((0, 0), (1, TAPS_MR - 1)))
    out = ((groups, TAPS_MR, 2 * TAPS_MR), jnp.bfloat16)
    return kernel_of(toeplitz_kernel, out)(taps)


def filter_kernel(
    qp_ref, kp_ref, vp_ref, qr_ref, kr_ref, vr_ref, taps_ref, toep_ref, out_ref, k_ref, v_ref, q_ref, g_ref
):
    rows, slab = out_ref.shape
    lane = lax.broadcasted_iota(jnp.int32, (2 * TAPS_MR, TILE), 1) // GROUP

    def filtered(ref, first, count, stream, start):
        total = None
        for by in range(TAPS_SHORT):
            tap = taps_ref[stream, pl.ds(by, 1), pl.ds(start, TILE)]
            term = tap * ref[pl.ds(first - by, count), :]
            total = term if total is None else total + term
        return total

    @pl.loop(0, slab // TILE)
    def _(tile):
        start = pl.multiple_of(tile * TILE, TILE)
        cols = pl.ds(start, TILE)
        k_ref[pl.ds(0, RIM), :] = kr_ref[:, cols].astype(jnp.float32)
        v_ref[pl.ds(0, RIM), :] = vr_ref[:, cols].astype(jnp.float32)
        q_ref[pl.ds(0, 8), :] = qr_ref[:, cols].astype(jnp.float32)[8:]
        k_ref[pl.ds(RIM, rows), :] = kp_ref[:, cols]
        v_ref[pl.ds(RIM, rows), :] = vp_ref[:, cols]
        q_ref[pl.ds(8, rows), :] = qp_ref[:, cols]
        for block in range((rows + TAPS_MR) // TAPS_MR):
            first = block * TAPS_MR + RIM - TAPS_MR
            gate = filtered(k_ref, first, TAPS_MR, 1, start) * filtered(v_ref, first, TAPS_MR, 2, start)
            g_ref[pl.ds(block * TAPS_MR, TAPS_MR), :] = gate.astype(jnp.bfloat16)
        for block in range(rows // TAPS_MR):
            window = g_ref[pl.ds(block * TAPS_MR, 2 * TAPS_MR), :]
            total = None
            for group in range(TILE // GROUP):
                picked = jnp.where(lane == group, window, jnp.zeros_like(window))
                term = jnp.dot(
                    toep_ref[tile * (TILE // GROUP) + group], picked, preferred_element_type=jnp.float32
                )
                total = term if total is None else total + term
            query = filtered(q_ref, 8 + block * TAPS_MR, TAPS_MR, 0, start)
            out_ref[pl.ds(block * TAPS_MR, TAPS_MR), pl.ds(start, TILE)] = (query * total).astype(jnp.bfloat16)


def filtering(q, k, v, q_rim, k_rim, v_rim, taps, toeplitz):
    rows, slab = q.shape
    scratch = [
        pltpu.VMEM((RIM + rows, TILE), jnp.float32),
        pltpu.VMEM((RIM + rows, TILE), jnp.float32),
        pltpu.VMEM((8 + rows, TILE), jnp.float32),
        pltpu.VMEM((TAPS_MR + rows, TILE), jnp.bfloat16),
    ]
    call = kernel_of(filter_kernel, ((rows, slab), jnp.bfloat16), scratch=scratch)
    return call(q, k, v, q_rim, k_rim, v_rim, taps, toeplitz)


def local(hidden, w_feature, short_filter, mr_filter, w_out):
    rows, feats = hidden.shape
    slab = w_feature.shape[2]
    ctx, tp = lax.axis_index("ctx"), lax.axis_index("tp")
    z, yl = tp // 2, tp % 2
    x, yh, core = ctx // 4, (ctx // 2) % 2, ctx % 2
    width = w_out.shape[1] // (2 * NZ)

    toeplitz = toeplitz_of(mr_filter)
    mine = send(hidden, swapped)

    w_own = w_feature.transpose(1, 0, 2)
    after = [send(w_own[p], along_x(-1)) for p in range(3)]
    before = [send(w_own[p], along_x(1)) for p in range(3)]
    far_k = send(after[1], along_x(-1))
    far_v = send(before[2], along_x(1))
    far_q0 = send(after[0][: feats // 2], along_x(-1))
    far_q1 = send(before[0][feats // 2 :], along_x(1))

    away = columns_of(jnp.stack([(core * 4 + t) * 2 + 1 - yl for t in range(4)]), w_out, width)
    shifts = (4, 3, -3, 2, -2, 1, -1, 0)
    to = jnp.stack([(z + by + NZ) % NZ for by in shifts])
    index = jnp.stack([(to // 4) ^ core, to % 4]).astype(jnp.int32)
    w_here = columns_of(to * 2 + yl, w_out, width)

    mine, toeplitz, away = lax.optimization_barrier((mine, toeplitz, away))
    w_near = send(away, other_yl)
    w_far = send(w_near, other_core)
    own = [mine, send(mine, other_yl)]
    t1, o1, t2, o2, t3, o3 = [], [], [], [], [], []
    for e in (0, 1):
        t1.append(send(own[e], to_partner))
        o1.append(send(own[e], to_other))
        t2.append(send(o1[e], to_partner))
        o2.append(send(t1[e], to_other))
        t3.append(send(o2[e], to_partner))
        o3.append(send(t2[e], to_other))
    o3[0], w_here = lax.optimization_barrier((o3[0], w_here))
    last = [send(o3[0], to_partner), send(t3[1], to_other)]

    held_order = []
    blocks = []
    for even, same, across in ((0, own, t1), (-1, o2, o1), (1, t2, t3), (2, last, o3)):
        by = even * (1 - 2 * (z % 2))
        for differs, pair in ((0, same), (1, across)):
            for e in (0, 1):
                part = (z // 2 + by - x + 2 * NX) % NX
                token = (yl ^ e ^ core) * 2 + ((z % 2) ^ differs ^ yh)
                held_order.append(part * 4 + token)
                blocks.append(pair[e])
    held_order = jnp.stack(held_order).astype(jnp.int32)
    held = kernel_of(arrange_kernel, ((16, rows, feats), jnp.bfloat16), 1)(held_order, *blocks)

    def stream_of(p):
        if p == 0:
            half = feats // 2
            lay = lambda r: (
                (0, r[0], 0, 0, feats),
                (1, r[1], None, 0, feats),
                (2, r[3], None, 0, half),
                (2, r[4], None, half, half),
                (3, r[2], None, 0, feats),
            )
            weights = (w_own, after[0], before[0], far_q0, far_q1)
        else:
            lay = lambda r: (
                (0, r[0], p, 0, feats),
                (1, r[1], None, 0, feats),
                (2, r[3], None, 0, feats),
                (3, r[2], None, 0, feats),
            )
            weights = (w_own, after[p], before[p], far_k if p == 1 else far_v)
        call = kernel_of(functools.partial(product_kernel, lay), ((4, rows, slab), jnp.bfloat16))
        partial = call(held, *weights)
        got = send(partial[2:], other_core)
        pair = partial[:2].astype(jnp.float32) + got.astype(jnp.float32)
        return pair[0] + send(pair[1].astype(jnp.bfloat16), other_yh).astype(jnp.float32)

    k, v, q = stream_of(1), stream_of(2), stream_of(0)
    k_rim = send(k[rows - RIM :].astype(jnp.bfloat16), next_block)
    v_rim = send(v[rows - RIM :].astype(jnp.bfloat16), next_block)
    q_rim = send(q[rows - 16 :].astype(jnp.bfloat16), next_block)
    mixer = filtering(q, k, v, q_rim, k_rim, v_rim, short_filter.transpose(1, 0, 2), toeplitz)
    mixer_other = send(mixer, other_yl)

    base = kernel_of(spread_own_kernel, ((8, rows, width), jnp.float32))(mixer, w_here)

    def spread(index, lo, count):
        call = kernel_of(
            functools.partial(spread_kernel, lo),
            ((count, rows, width), jnp.float32),
            1,
            [pltpu.VMEM((feats, width), jnp.bfloat16)],
        )
        return call(index, mixer_other, w_near, w_far, base)

    early = spread(index, 0, 3)
    later, early = lax.optimization_barrier((index, early))
    late = spread(later, 3, 5)
    part = {by: early[i] if i < 3 else late[i - 3] for i, by in enumerate(shifts)}
    half = width // 2
    cols = [slice(0, half), slice(half, width)]
    ups = [part[4][:, cols[0]].astype(jnp.bfloat16), None]
    downs = [None, part[4][:, cols[1]].astype(jnp.bfloat16)]
    for step in range(1, 5):
        ups = [None if u is None else send(u, along_z(1)) for u in ups]
        downs = [None if d is None else send(d, along_z(-1)) for d in downs]
        if step == 4:
            break
        for h in (0, 1):
            up, down = part[4 - step][:, cols[h]], part[step - 4][:, cols[h]]
            if ups[h] is not None:
                up = up + ups[h].astype(jnp.float32)
            if downs[h] is not None:
                down = down + downs[h].astype(jnp.float32)
            ups[h], downs[h] = up.astype(jnp.bfloat16), down.astype(jnp.bfloat16)
    sums = [
        part[0][:, cols[h]] + ups[h].astype(jnp.float32) + downs[h].astype(jnp.float32) for h in (0, 1)
    ]
    return jnp.concatenate(sums, 1).astype(jnp.bfloat16)


def solution(mesh):
    return jax.shard_map(
        local,
        mesh=mesh,
        in_specs=(
            P("ctx", "tp"),
            P("ctx", None, "tp"),
            P(None, None, "tp"),
            P("tp", None),
            P("tp", None),
        ),
        out_specs=P("ctx", "tp"),
        check_vma=False,
    )
```

```python
import functools

import jax
import jax.numpy as jnp
from jax import lax
from jax.experimental import pallas as pl
from jax.experimental.pallas import tpu as pltpu
from jax.sharding import PartitionSpec as P

TAPS_SHORT = 7
TAPS_MR = 128
GROUP = 16
NX, NZ = 4, 8
RIM = 136
TILE = 256


def pairs_of(move):
    out = []
    for x in range(NX):
        for yh in range(2):
            for core in range(2):
                for z in range(NZ):
                    for yl in range(2):
                        to = move(x, yh, core, z, yl)
                        if to is None:
                            continue
                        tx, tyh, tcore, tz, tyl = to
                        here = ((x * 2 + yh) * 2 + core) * 16 + z * 2 + yl
                        there = ((tx * 2 + tyh) * 2 + tcore) * 16 + tz * 2 + tyl
                        out.append((here, there))
    return out


def send(value, move):
    return lax.ppermute(value, ("ctx", "tp"), pairs_of(move))


def along_x(by):
    return lambda x, yh, core, z, yl: ((x + by) % NX, yh, core, z, yl)


def along_z(by):
    return lambda x, yh, core, z, yl: (x, yh, core, (z + by) % NZ, yl)


def other_yh(x, yh, core, z, yl):
    return x, 1 - yh, core, z, yl


def other_core(x, yh, core, z, yl):
    return x, yh, 1 - core, z, yl


def other_yl(x, yh, core, z, yl):
    return x, yh, core, z, 1 - yl


def swapped(x, yh, core, z, yl):
    return x, z % 2, yl, z - z % 2 + yh, core


def to_partner(x, yh, core, z, yl):
    return x, yh, core, z ^ 1, yl


def to_other(x, yh, core, z, yl):
    return x, yh, core, (z + (1 if z % 2 else -1)) % NZ, yl


def next_block(x, yh, core, z, yl):
    block = (x * 2 + yh) * 2 + core + 1
    if block == 16:
        return None
    return block // 4, (block // 2) % 2, block % 2, z, yl


def in_vmem(value):
    return pltpu.with_memory_space_constraint(value, pltpu.VMEM)


def kernel_of(body, out, scalars=0, scratch=(), limit=8):
    whole = pl.BlockSpec(memory_space=pltpu.VMEM)

    def call(*args):
        placed = [*args[:scalars], *(in_vmem(a) for a in args[scalars:])]
        return pl.pallas_call(
            body,
            out_shape=pltpu.VMEM(*out),
            in_specs=[pl.BlockSpec(memory_space=pltpu.SMEM)] * scalars + [whole] * (len(args) - scalars),
            out_specs=whole,
            scratch_shapes=list(scratch),
            compiler_params=pltpu.CompilerParams(vmem_limit_bytes=limit << 20),
        )(*placed)

    return call


def arrange_kernel(order_ref, *refs):
    out_ref = refs[-1]
    for slot, ref in enumerate(refs[:-1]):
        out_ref[order_ref[slot]] = ref[...]


def product_kernel(stream_ref, held_ref, *refs):
    out_ref = refs[-1]
    depth = held_ref.shape[2]
    stream = stream_ref[0]

    @pl.loop(0, 4)
    def _(token):
        total = None
        for part, ref, lo in zip((0, 1, 2, 2, 3), refs[:-1], (0, 0, 0, depth // 2, 0)):
            left = held_ref[part * 4 + token, :, pl.ds(lo, ref.shape[1])]
            term = jnp.dot(left, ref[stream], preferred_element_type=jnp.float32)
            total = term if total is None else total + term
        out_ref[token] = total.astype(jnp.bfloat16)


def columns_kernel(at_ref, w_ref, out_ref, sems):
    width = out_ref.shape[2]
    copies = []
    for i in range(out_ref.shape[0]):
        cols = pl.ds(pl.multiple_of(at_ref[i] * width, width), width)
        copies.append(pltpu.make_async_copy(w_ref.at[:, cols], out_ref.at[i], sems.at[i]))
        copies[-1].start()
    for copy in copies:
        copy.wait()


def columns_of(at, w, width):
    count = at.shape[0]
    return pl.pallas_call(
        columns_kernel,
        out_shape=pltpu.VMEM((count, w.shape[0], width), w.dtype),
        in_specs=[pl.BlockSpec(memory_space=pltpu.SMEM), pl.BlockSpec(memory_space=pltpu.HBM)],
        out_specs=pl.BlockSpec(memory_space=pltpu.VMEM),
        scratch_shapes=[pltpu.SemaphoreType.DMA((count,))],
        compiler_params=pltpu.CompilerParams(vmem_limit_bytes=8 << 20),
        name="columns",
    )(at.astype(jnp.int32), pltpu.with_memory_space_constraint(w, pltpu.HBM))


def spread_own_kernel(own_ref, w_ref, out_ref):
    @pl.loop(0, out_ref.shape[0])
    def _(i):
        out_ref[i] = jnp.dot(own_ref[...], w_ref[i], preferred_element_type=jnp.float32)


def spread_kernel(lo, index_ref, other_ref, near_ref, far_ref, base_ref, out_ref, held):
    @pl.loop(0, out_ref.shape[0])
    def _(i):
        to = index_ref[1, lo + i]

        @pl.when(index_ref[0, lo + i] == 0)
        def _():
            held[...] = near_ref[to]

        @pl.when(index_ref[0, lo + i] != 0)
        def _():
            held[...] = far_ref[to]

        out_ref[i] = base_ref[lo + i] + jnp.dot(
            other_ref[...], held[...], preferred_element_type=jnp.float32
        )


def toeplitz_kernel(taps_ref, out_ref):
    @pl.loop(0, out_ref.shape[0])
    def _(group):
        row = jnp.broadcast_to(taps_ref[pl.ds(group, 1), :], (TAPS_MR, 2 * TAPS_MR))
        out_ref[group] = pltpu.roll(row, 0, 1, stride=1, stride_axis=0).astype(jnp.bfloat16)


def toeplitz_of(filters):
    groups = filters.shape[0]
    taps = jnp.pad(filters[:, ::-1].astype(jnp.float32), ((0, 0), (1, TAPS_MR - 1)))
    out = ((groups, TAPS_MR, 2 * TAPS_MR), jnp.bfloat16)
    return kernel_of(toeplitz_kernel, out)(taps)


def filter_kernel(
    qp_ref, kp_ref, vp_ref, qr_ref, kr_ref, vr_ref, taps_ref, toep_ref, out_ref, k_ref, v_ref, q_ref, g_ref
):
    rows, slab = out_ref.shape
    lane = lax.broadcasted_iota(jnp.int32, (2 * TAPS_MR, TILE), 1) // GROUP

    def filtered(ref, first, count, stream, start):
        total = None
        for by in range(TAPS_SHORT):
            tap = taps_ref[stream, pl.ds(by, 1), pl.ds(start, TILE)]
            term = tap * ref[pl.ds(first - by, count), :]
            total = term if total is None else total + term
        return total

    @pl.loop(0, slab // TILE)
    def _(tile):
        start = pl.multiple_of(tile * TILE, TILE)
        cols = pl.ds(start, TILE)
        k_ref[pl.ds(0, RIM), :] = kr_ref[:, cols].astype(jnp.float32)
        v_ref[pl.ds(0, RIM), :] = vr_ref[:, cols].astype(jnp.float32)
        q_ref[pl.ds(0, 8), :] = qr_ref[:, cols].astype(jnp.float32)[8:]
        k_ref[pl.ds(RIM, rows), :] = kp_ref[:, cols]
        v_ref[pl.ds(RIM, rows), :] = vp_ref[:, cols]
        q_ref[pl.ds(8, rows), :] = qp_ref[:, cols]
        for block in range((rows + TAPS_MR) // TAPS_MR):
            first = block * TAPS_MR + RIM - TAPS_MR
            gate = filtered(k_ref, first, TAPS_MR, 1, start) * filtered(v_ref, first, TAPS_MR, 2, start)
            g_ref[pl.ds(block * TAPS_MR, TAPS_MR), :] = gate.astype(jnp.bfloat16)
        for block in range(rows // TAPS_MR):
            window = g_ref[pl.ds(block * TAPS_MR, 2 * TAPS_MR), :]
            total = None
            for group in range(TILE // GROUP):
                picked = jnp.where(lane == group, window, jnp.zeros_like(window))
                term = jnp.dot(
                    toep_ref[tile * (TILE // GROUP) + group], picked, preferred_element_type=jnp.float32
                )
                total = term if total is None else total + term
            query = filtered(q_ref, 8 + block * TAPS_MR, TAPS_MR, 0, start)
            out_ref[pl.ds(block * TAPS_MR, TAPS_MR), pl.ds(start, TILE)] = (query * total).astype(jnp.bfloat16)


def filtering(q, k, v, q_rim, k_rim, v_rim, taps, toeplitz):
    rows, slab = q.shape
    scratch = [
        pltpu.VMEM((RIM + rows, TILE), jnp.float32),
        pltpu.VMEM((RIM + rows, TILE), jnp.float32),
        pltpu.VMEM((8 + rows, TILE), jnp.float32),
        pltpu.VMEM((TAPS_MR + rows, TILE), jnp.bfloat16),
    ]
    call = kernel_of(filter_kernel, ((rows, slab), jnp.bfloat16), scratch=scratch, limit=10)
    return call(q, k, v, q_rim, k_rim, v_rim, taps, toeplitz)


def local(hidden, w_feature, short_filter, mr_filter, w_out):
    rows, feats = hidden.shape
    slab = w_feature.shape[2]
    ctx, tp = lax.axis_index("ctx"), lax.axis_index("tp")
    z, yl = tp // 2, tp % 2
    x, yh, core = ctx // 4, (ctx // 2) % 2, ctx % 2
    width = w_out.shape[1] // (2 * NZ)

    toeplitz = toeplitz_of(mr_filter)
    mine = send(hidden, swapped)

    w_own = w_feature.transpose(1, 0, 2)
    after = send(w_own, along_x(-1))
    before = send(w_own, along_x(1))
    far_lo = send(after[:, : feats // 2], along_x(-1))
    far_hi = send(before[:, feats // 2 :], along_x(1))
    weights = (w_own, after, far_lo, far_hi, before)

    away = columns_of(jnp.stack([(core * 4 + t) * 2 + 1 - yl for t in range(4)]), w_out, width)
    shifts = (4, 3, -3, 2, -2, 1, -1, 0)
    to = jnp.stack([(z + by + NZ) % NZ for by in shifts])
    index = jnp.stack([(to // 4) ^ core, to % 4]).astype(jnp.int32)
    w_here = columns_of(to * 2 + yl, w_out, width)

    w_near = send(away, other_yl)
    w_far = send(w_near, other_core)
    own = [mine, send(mine, other_yl)]
    t1, o1, t2, o2, t3, o3 = [], [], [], [], [], []
    for e in (0, 1):
        t1.append(send(own[e], to_partner))
        o1.append(send(own[e], to_other))
        t2.append(send(o1[e], to_partner))
        o2.append(send(t1[e], to_other))
        t3.append(send(o2[e], to_partner))
        o3.append(send(t2[e], to_other))
    o3[0], w_here, toeplitz = lax.optimization_barrier((o3[0], w_here, toeplitz))
    last = [send(o3[0], to_partner), send(t3[1], to_other)]

    held_order = []
    blocks = []
    for even, same, across in ((0, own, t1), (-1, o2, o1), (1, t2, t3), (2, last, o3)):
        by = even * (1 - 2 * (z % 2))
        for differs, pair in ((0, same), (1, across)):
            for e in (0, 1):
                part = (z // 2 + by - x + 2 * NX) % NX
                token = (yl ^ e ^ core) * 2 + ((z % 2) ^ differs ^ yh)
                held_order.append(part * 4 + token)
                blocks.append(pair[e])
    held_order = jnp.stack(held_order).astype(jnp.int32)
    held = kernel_of(arrange_kernel, ((16, rows, feats), jnp.bfloat16), 1)(held_order, *blocks)

    def stream_of(p):
        out = ((4, rows, slab), jnp.bfloat16)
        call = kernel_of(product_kernel, out, 1, limit=14)
        partial = call(jnp.full((1,), p, jnp.int32), held, *weights)
        got = send(partial[2:], other_core)
        pair = partial[:2].astype(jnp.float32) + got.astype(jnp.float32)
        return pair[0] + send(pair[1].astype(jnp.bfloat16), other_yh).astype(jnp.float32)

    k, v, q = stream_of(1), stream_of(2), stream_of(0)
    k_rim = send(k[rows - RIM :].astype(jnp.bfloat16), next_block)
    v_rim = send(v[rows - RIM :].astype(jnp.bfloat16), next_block)
    q_rim = send(q[rows - 16 :].astype(jnp.bfloat16), next_block)
    mixer = filtering(q, k, v, q_rim, k_rim, v_rim, short_filter.transpose(1, 0, 2), toeplitz)
    mixer_other = send(mixer, other_yl)

    base = kernel_of(spread_own_kernel, ((8, rows, width), jnp.float32), limit=14)(mixer, w_here)

    def spread(index, lo, count):
        call = kernel_of(
            functools.partial(spread_kernel, lo),
            ((count, rows, width), jnp.float32),
            1,
            [pltpu.VMEM((feats, width), jnp.bfloat16)],
            limit=14,
        )
        return call(index, mixer_other, w_near, w_far, base)

    early = spread(index, 0, 3)
    late = spread(index, 3, 5)
    part = {by: early[i] if i < 3 else late[i - 3] for i, by in enumerate(shifts)}
    half = width // 2
    cols = [slice(0, half), slice(half, width)]
    ups = [part[4][:, cols[0]].astype(jnp.bfloat16), None]
    downs = [None, part[4][:, cols[1]].astype(jnp.bfloat16)]
    for step in range(1, 5):
        ups = [None if u is None else send(u, along_z(1)) for u in ups]
        downs = [None if d is None else send(d, along_z(-1)) for d in downs]
        if step == 4:
            break
        for h in (0, 1):
            up, down = part[4 - step][:, cols[h]], part[step - 4][:, cols[h]]
            if ups[h] is not None:
                up = up + ups[h].astype(jnp.float32)
            if downs[h] is not None:
                down = down + downs[h].astype(jnp.float32)
            ups[h], downs[h] = up.astype(jnp.bfloat16), down.astype(jnp.bfloat16)
    sums = [
        part[0][:, cols[h]] + ups[h].astype(jnp.float32) + downs[h].astype(jnp.float32) for h in (0, 1)
    ]
    return jnp.concatenate(sums, 1).astype(jnp.bfloat16)


def solution(mesh):
    return jax.shard_map(
        local,
        mesh=mesh,
        in_specs=(
            P("ctx", "tp"),
            P("ctx", None, "tp"),
            P(None, None, "tp"),
            P("tp", None),
            P("tp", None),
        ),
        out_specs=P("ctx", "tp"),
        check_vma=False,
    )
```

```python
import functools

import jax
import jax.numpy as jnp
import numpy as np
from jax import lax
from jax.experimental import pallas as pl
from jax.experimental.pallas import tpu as pltpu
from jax.sharding import PartitionSpec as P

TAPS_SHORT = 7
TAPS_MR = 128
GROUP = 16
NX, NZ = 4, 8
RIM = 136
TILE = 256


def pairs_of(move):
    out = []
    for x in range(NX):
        for yh in range(2):
            for core in range(2):
                for z in range(NZ):
                    for yl in range(2):
                        to = move(x, yh, core, z, yl)
                        if to is None:
                            continue
                        tx, tyh, tcore, tz, tyl = to
                        here = ((x * 2 + yh) * 2 + core) * 16 + z * 2 + yl
                        there = ((tx * 2 + tyh) * 2 + tcore) * 16 + tz * 2 + tyl
                        out.append((here, there))
    return out


SHIFTS = (4, 3, -3, 2, -2, 1, -1, 0)
ORDER_AT, HERE_AT, SIDE_AT, PLACE_AT, AWAY_AT, COUNT = 0, 16, 24, 32, 40, 128


def tables():
    rows = np.zeros((256, COUNT), np.int32)
    for device in range(256):
        ctx, tp = divmod(device, 16)
        x, yh, core, z, yl = ctx // 4, (ctx // 2) % 2, ctx % 2, tp // 2, tp % 2
        row = []
        for even in (0, -1, 1, 2):
            by = even * (1 - 2 * (z % 2))
            for differs in (0, 1):
                for e in (0, 1):
                    token = (yl ^ e ^ core) * 2 + ((z % 2) ^ differs ^ yh)
                    row.append(((z // 2 + by - x) % NX) * 4 + token)
        to = [(z + by) % NZ for by in SHIFTS]
        row += [t * 2 + yl for t in to] + [(t // 4) ^ core for t in to] + [t % 4 for t in to]
        row += [(core * 4 + t) * 2 + 1 - yl for t in range(4)]
        rows[device, : len(row)] = row
    return rows


def send(value, move):
    return lax.ppermute(value, ("ctx", "tp"), pairs_of(move))


def along_x(by):
    return lambda x, yh, core, z, yl: ((x + by) % NX, yh, core, z, yl)


def along_z(by):
    return lambda x, yh, core, z, yl: (x, yh, core, (z + by) % NZ, yl)


def other_yh(x, yh, core, z, yl):
    return x, 1 - yh, core, z, yl


def other_core(x, yh, core, z, yl):
    return x, yh, 1 - core, z, yl


def other_yl(x, yh, core, z, yl):
    return x, yh, core, z, 1 - yl


def swapped(x, yh, core, z, yl):
    return x, z % 2, yl, z - z % 2 + yh, core


def to_partner(x, yh, core, z, yl):
    return x, yh, core, z ^ 1, yl


def to_other(x, yh, core, z, yl):
    return x, yh, core, (z + (1 if z % 2 else -1)) % NZ, yl


def next_block(x, yh, core, z, yl):
    block = (x * 2 + yh) * 2 + core + 1
    if block == 16:
        return None
    return block // 4, (block // 2) % 2, block % 2, z, yl


def in_vmem(value):
    return pltpu.with_memory_space_constraint(value, pltpu.VMEM)


def kernel_of(body, out, scalars=0, scratch=(), limit=8):
    whole = pl.BlockSpec(memory_space=pltpu.VMEM)

    def call(*args):
        placed = [*args[:scalars], *(in_vmem(a) for a in args[scalars:])]
        return pl.pallas_call(
            body,
            out_shape=pltpu.VMEM(*out),
            in_specs=[pl.BlockSpec(memory_space=pltpu.SMEM)] * scalars + [whole] * (len(args) - scalars),
            out_specs=whole,
            scratch_shapes=list(scratch),
            compiler_params=pltpu.CompilerParams(vmem_limit_bytes=limit << 20),
        )(*placed)

    return call


def join_kernel(lo_ref, hi_ref, out_ref):
    half = lo_ref.shape[1]
    out_ref[:, :half, :] = lo_ref[...]
    out_ref[:, half:, :] = hi_ref[...]


def arrange_kernel(order_ref, *refs):
    out_ref = refs[-1]
    for slot, ref in enumerate(refs[:-1]):
        out_ref[order_ref[ORDER_AT + slot]] = ref[...]


def product_kernel(stream_ref, held_ref, *refs):
    out_ref = refs[-1]
    stream = stream_ref[0]

    @pl.loop(0, 4)
    def _(token):
        total = None
        for part, ref in enumerate(refs[:-1]):
            term = jnp.dot(held_ref[part * 4 + token], ref[stream], preferred_element_type=jnp.float32)
            total = term if total is None else total + term
        out_ref[token] = total.astype(jnp.bfloat16)


def columns_kernel(at_ref, w_ref, out_ref, sems):
    width = out_ref.shape[2]
    copies = []
    for i in range(out_ref.shape[0]):
        cols = pl.ds(pl.multiple_of(at_ref[AWAY_AT + i] * width, width), width)
        copies.append(pltpu.make_async_copy(w_ref.at[:, cols], out_ref.at[i], sems.at[i]))
        copies[-1].start()
    for copy in copies:
        copy.wait()


def columns_of(at, w, count, width):
    return pl.pallas_call(
        columns_kernel,
        out_shape=pltpu.VMEM((count, w.shape[0], width), w.dtype),
        in_specs=[pl.BlockSpec(memory_space=pltpu.SMEM), pl.BlockSpec(memory_space=pltpu.HBM)],
        out_specs=pl.BlockSpec(memory_space=pltpu.VMEM),
        scratch_shapes=[pltpu.SemaphoreType.DMA((count,))],
        compiler_params=pltpu.CompilerParams(vmem_limit_bytes=8 << 20),
        name="columns",
    )(at, pltpu.with_memory_space_constraint(w, pltpu.HBM))


def spread_own_kernel(at_ref, own_ref, w_ref, out_ref):
    out_ref[0] = jnp.dot(own_ref[...], w_ref[...], preferred_element_type=jnp.float32)


def spread_own(at, own, w, width):
    rows, depth = own.shape
    count = len(SHIFTS)
    return pl.pallas_call(
        spread_own_kernel,
        out_shape=pltpu.VMEM((count, rows, width), jnp.float32),
        grid_spec=pltpu.PrefetchScalarGridSpec(
            num_scalar_prefetch=1,
            grid=(count,),
            in_specs=[
                pl.BlockSpec((rows, depth), lambda i, at: (0, 0)),
                pl.BlockSpec((depth, width), lambda i, at: (0, at[HERE_AT + i])),
            ],
            out_specs=pl.BlockSpec((1, rows, width), lambda i, at: (i, 0, 0)),
        ),
        compiler_params=pltpu.CompilerParams(vmem_limit_bytes=8 << 20),
        name="spread_own",
    )(at, own, pltpu.with_memory_space_constraint(w, pltpu.HBM))


def spread_kernel(lo, index_ref, other_ref, near_ref, far_ref, base_ref, out_ref, held):
    @pl.loop(0, out_ref.shape[0])
    def _(i):
        to, side = index_ref[PLACE_AT + lo + i], index_ref[SIDE_AT + lo + i]

        @pl.when(side == 0)
        def _():
            held[...] = near_ref[to]

        @pl.when(side != 0)
        def _():
            held[...] = far_ref[to]

        out_ref[i] = base_ref[lo + i] + jnp.dot(
            other_ref[...], held[...], preferred_element_type=jnp.float32
        )


def toeplitz_kernel(mr_ref, out_ref, taps_ref):
    shape = (TAPS_MR, 2 * TAPS_MR)
    from_tap = lax.broadcasted_iota(jnp.int32, shape, 0)
    to_lane = lax.broadcasted_iota(jnp.int32, shape, 1)
    flip = jnp.where(from_tap + to_lane == TAPS_MR, 1.0, 0.0).astype(jnp.bfloat16)
    taps_ref[...] = jnp.dot(mr_ref[...], flip, preferred_element_type=jnp.float32)

    @pl.loop(0, out_ref.shape[0])
    def _(group):
        row = jnp.broadcast_to(taps_ref[pl.ds(group, 1), :], shape)
        out_ref[group] = pltpu.roll(row, 0, 1, stride=1, stride_axis=0).astype(jnp.bfloat16)


def toeplitz_of(filters):
    groups = filters.shape[0]
    out = ((groups, TAPS_MR, 2 * TAPS_MR), jnp.bfloat16)
    scratch = [pltpu.VMEM((groups, 2 * TAPS_MR), jnp.float32)]
    return kernel_of(toeplitz_kernel, out, scratch=scratch)(filters)


def filter_kernel(
    qp_ref, kp_ref, vp_ref, qr_ref, kvr_ref, taps_ref, toep_ref, out_ref, k_ref, v_ref, q_ref, g_ref
):
    rows, slab = out_ref.shape
    lane = lax.broadcasted_iota(jnp.int32, (2 * TAPS_MR, TILE), 1) // GROUP

    def filtered(ref, first, count, stream, start):
        total = None
        for by in range(TAPS_SHORT):
            tap = taps_ref[stream, pl.ds(by, 1), pl.ds(start, TILE)]
            term = tap * ref[pl.ds(first - by, count), :]
            total = term if total is None else total + term
        return total

    @pl.loop(0, slab // TILE)
    def _(tile):
        start = pl.multiple_of(tile * TILE, TILE)
        cols = pl.ds(start, TILE)
        k_ref[pl.ds(0, RIM), :] = kvr_ref[0, :, cols].astype(jnp.float32)
        v_ref[pl.ds(0, RIM), :] = kvr_ref[1, :, cols].astype(jnp.float32)
        q_ref[pl.ds(0, 8), :] = qr_ref[:, cols].astype(jnp.float32)[8:]
        k_ref[pl.ds(RIM, rows), :] = kp_ref[:, cols]
        v_ref[pl.ds(RIM, rows), :] = vp_ref[:, cols]
        q_ref[pl.ds(8, rows), :] = qp_ref[:, cols]
        for block in range((rows + TAPS_MR) // TAPS_MR):
            first = block * TAPS_MR + RIM - TAPS_MR
            gate = filtered(k_ref, first, TAPS_MR, 1, start) * filtered(v_ref, first, TAPS_MR, 2, start)
            g_ref[pl.ds(block * TAPS_MR, TAPS_MR), :] = gate.astype(jnp.bfloat16)
        for block in range(rows // TAPS_MR):
            window = g_ref[pl.ds(block * TAPS_MR, 2 * TAPS_MR), :]
            total = None
            for group in range(TILE // GROUP):
                picked = jnp.where(lane == group, window, jnp.zeros_like(window))
                term = jnp.dot(
                    toep_ref[tile * (TILE // GROUP) + group], picked, preferred_element_type=jnp.float32
                )
                total = term if total is None else total + term
            query = filtered(q_ref, 8 + block * TAPS_MR, TAPS_MR, 0, start)
            out_ref[pl.ds(block * TAPS_MR, TAPS_MR), pl.ds(start, TILE)] = (query * total).astype(jnp.bfloat16)


def filtering(q, k, v, q_rim, kv_rim, taps, toeplitz):
    rows, slab = q.shape
    scratch = [
        pltpu.VMEM((RIM + rows, TILE), jnp.float32),
        pltpu.VMEM((RIM + rows, TILE), jnp.float32),
        pltpu.VMEM((8 + rows, TILE), jnp.float32),
        pltpu.VMEM((TAPS_MR + rows, TILE), jnp.bfloat16),
    ]
    call = kernel_of(filter_kernel, ((rows, slab), jnp.bfloat16), scratch=scratch, limit=10)
    return call(q, k, v, q_rim, kv_rim, taps, toeplitz)


def local(hidden, w_feature, short_filter, mr_filter, w_out):
    rows, feats = hidden.shape
    slab = w_feature.shape[2]
    width = w_out.shape[1] // (2 * NZ)
    device = lax.axis_index("ctx") * 16 + lax.axis_index("tp")
    table = lax.dynamic_slice_in_dim(jnp.asarray(tables()), device, 1, 0)[0]

    toeplitz = toeplitz_of(mr_filter)
    mine = send(hidden, swapped)
    mine, table = lax.optimization_barrier((mine, table))

    w_own = w_feature.transpose(1, 0, 2)
    after = send(w_own, along_x(-1))
    before = send(w_own, along_x(1))
    far_lo = send(after[:, : feats // 2], along_x(-1))
    far_hi = send(before[:, feats // 2 :], along_x(1))
    far = kernel_of(join_kernel, ((3, feats, slab), jnp.bfloat16))(far_lo, far_hi)
    weights = (w_own, after, far, before)

    away = columns_of(table, w_out, 4, width)
    w_near = send(away, other_yl)
    w_far = send(w_near, other_core)
    own = [mine, send(mine, other_yl)]
    t1, o1, t2, o2, t3, o3 = [], [], [], [], [], []
    for e in (0, 1):
        t1.append(send(own[e], to_partner))
        o1.append(send(own[e], to_other))
        t2.append(send(o1[e], to_partner))
        o2.append(send(t1[e], to_other))
        t3.append(send(o2[e], to_partner))
        o3.append(send(t2[e], to_other))
    last = [send(o3[0], to_partner), send(t3[1], to_other)]

    blocks = [b for pair in (own, t1, o2, o1, t2, t3, last, o3) for b in pair]
    held = kernel_of(arrange_kernel, ((16, rows, feats), jnp.bfloat16), 1)(table, *blocks)

    def stream_of(p):
        out = ((4, rows, slab), jnp.bfloat16)
        call = kernel_of(product_kernel, out, 1, limit=14)
        partial = call(jnp.full((1,), p, jnp.int32), held, *weights)
        got = send(partial[2:], other_core)
        pair = partial[:2].astype(jnp.float32) + got.astype(jnp.float32)
        return pair[0] + send(pair[1].astype(jnp.bfloat16), other_yh).astype(jnp.float32)

    k, v, q = stream_of(1), stream_of(2), stream_of(0)
    kv_rim = jnp.stack([k[rows - RIM :], v[rows - RIM :]]).astype(jnp.bfloat16)
    kv_rim = send(kv_rim, next_block)
    q_rim = send(q[rows - 16 :].astype(jnp.bfloat16), next_block)
    mixer = filtering(q, k, v, q_rim, kv_rim, short_filter.transpose(1, 0, 2), toeplitz)
    mixer_other = send(mixer, other_yl)

    base = spread_own(table, mixer, w_out, width)

    def spread(lo, count):
        call = kernel_of(
            functools.partial(spread_kernel, lo),
            ((count, rows, width), jnp.float32),
            1,
            [pltpu.VMEM((feats, width), jnp.bfloat16)],
            limit=14,
        )
        return call(table, mixer_other, w_near, w_far, base)

    early = spread(0, 3)
    late = spread(3, 5)
    part = {by: early[i] if i < 3 else late[i - 3] for i, by in enumerate(SHIFTS)}
    half = width // 2
    cols = [slice(0, half), slice(half, width)]
    ups = [part[4][:, cols[0]].astype(jnp.bfloat16), None]
    downs = [None, part[4][:, cols[1]].astype(jnp.bfloat16)]
    for step in range(1, 5):
        ups = [None if u is None else send(u, along_z(1)) for u in ups]
        downs = [None if d is None else send(d, along_z(-1)) for d in downs]
        if step == 4:
            break
        for h in (0, 1):
            up, down = part[4 - step][:, cols[h]], part[step - 4][:, cols[h]]
            if ups[h] is not None:
                up = up + ups[h].astype(jnp.float32)
            if downs[h] is not None:
                down = down + downs[h].astype(jnp.float32)
            ups[h], downs[h] = up.astype(jnp.bfloat16), down.astype(jnp.bfloat16)
    sums = [
        part[0][:, cols[h]] + ups[h].astype(jnp.float32) + downs[h].astype(jnp.float32) for h in (0, 1)
    ]
    return jnp.concatenate(sums, 1).astype(jnp.bfloat16)


def solution(mesh):
    return jax.shard_map(
        local,
        mesh=mesh,
        in_specs=(
            P("ctx", "tp"),
            P("ctx", None, "tp"),
            P(None, None, "tp"),
            P("tp", None),
            P("tp", None),
        ),
        out_specs=P("ctx", "tp"),
        check_vma=False,
    )
```

```python
import functools

import jax
import jax.numpy as jnp
import numpy as np
from jax import lax
from jax.experimental import pallas as pl
from jax.experimental.pallas import tpu as pltpu
from jax.sharding import PartitionSpec as P

TAPS_SHORT = 7
TAPS_MR = 128
GROUP = 16
NX, NZ = 4, 8
RIM = 136
TILE = 256


def pairs_of(move):
    out = []
    for x in range(NX):
        for yh in range(2):
            for core in range(2):
                for z in range(NZ):
                    for yl in range(2):
                        to = move(x, yh, core, z, yl)
                        if to is None:
                            continue
                        tx, tyh, tcore, tz, tyl = to
                        here = ((x * 2 + yh) * 2 + core) * 16 + z * 2 + yl
                        there = ((tx * 2 + tyh) * 2 + tcore) * 16 + tz * 2 + tyl
                        out.append((here, there))
    return out


SHIFTS = (4, 3, -3, 2, -2, 1, -1, 0)
ORDER_AT, HERE_AT, SIDE_AT, PLACE_AT, AWAY_AT, COUNT = 0, 16, 24, 32, 40, 128


def tables():
    rows = np.zeros((256, COUNT), np.int32)
    for device in range(256):
        ctx, tp = divmod(device, 16)
        x, yh, core, z, yl = ctx // 4, (ctx // 2) % 2, ctx % 2, tp // 2, tp % 2
        row = []
        for even in (0, -1, 1, 2):
            by = even * (1 - 2 * (z % 2))
            for differs in (0, 1):
                for e in (0, 1):
                    token = (yl ^ e ^ core) * 2 + ((z % 2) ^ differs ^ yh)
                    row.append(((z // 2 + by - x) % NX) * 4 + token)
        to = [(z + by) % NZ for by in SHIFTS]
        row += [t * 2 + yl for t in to] + [(t // 4) ^ core for t in to] + [t % 4 for t in to]
        row += [(core * 4 + t) * 2 + 1 - yl for t in range(4)]
        rows[device, : len(row)] = row
    return rows


def send(value, move):
    return lax.ppermute(value, ("ctx", "tp"), pairs_of(move))


def along_x(by):
    return lambda x, yh, core, z, yl: ((x + by) % NX, yh, core, z, yl)


def along_z(by):
    return lambda x, yh, core, z, yl: (x, yh, core, (z + by) % NZ, yl)


def other_yh(x, yh, core, z, yl):
    return x, 1 - yh, core, z, yl


def other_core(x, yh, core, z, yl):
    return x, yh, 1 - core, z, yl


def other_yl(x, yh, core, z, yl):
    return x, yh, core, z, 1 - yl


def swapped(x, yh, core, z, yl):
    return x, z % 2, yl, z - z % 2 + yh, core


def to_partner(x, yh, core, z, yl):
    return x, yh, core, z ^ 1, yl


def to_other(x, yh, core, z, yl):
    return x, yh, core, (z + (1 if z % 2 else -1)) % NZ, yl


def next_block(x, yh, core, z, yl):
    block = (x * 2 + yh) * 2 + core + 1
    if block == 16:
        return None
    return block // 4, (block // 2) % 2, block % 2, z, yl


def in_vmem(value):
    return pltpu.with_memory_space_constraint(value, pltpu.VMEM)


def kernel_of(body, out, scalars=0, scratch=(), limit=8):
    whole = pl.BlockSpec(memory_space=pltpu.VMEM)

    def call(*args):
        placed = [*args[:scalars], *(in_vmem(a) for a in args[scalars:])]
        return pl.pallas_call(
            body,
            out_shape=pltpu.VMEM(*out),
            in_specs=[pl.BlockSpec(memory_space=pltpu.SMEM)] * scalars + [whole] * (len(args) - scalars),
            out_specs=whole,
            scratch_shapes=list(scratch),
            compiler_params=pltpu.CompilerParams(vmem_limit_bytes=limit << 20),
        )(*placed)

    return call


def join_kernel(lo_ref, hi_ref, out_ref):
    half = lo_ref.shape[1]
    out_ref[:, :half, :] = lo_ref[...]
    out_ref[:, half:, :] = hi_ref[...]


def arrange_kernel(order_ref, *refs):
    out_ref = refs[-1]
    for slot, ref in enumerate(refs[:-1]):
        out_ref[order_ref[ORDER_AT + slot]] = ref[...]


def product_kernel(stream_ref, held_ref, *refs):
    out_ref = refs[-1]
    stream = stream_ref[0]

    @pl.loop(0, 4)
    def _(token):
        total = None
        for part, ref in enumerate(refs[:-1]):
            term = jnp.dot(held_ref[part * 4 + token], ref[stream], preferred_element_type=jnp.float32)
            total = term if total is None else total + term
        out_ref[token] = total.astype(jnp.bfloat16)


def columns_kernel(first, at_ref, w_ref, out_ref, sems):
    width = out_ref.shape[2]
    copies = []
    for i in range(out_ref.shape[0]):
        cols = pl.ds(pl.multiple_of(at_ref[AWAY_AT + first + i] * width, width), width)
        copies.append(pltpu.make_async_copy(w_ref.at[:, cols], out_ref.at[i], sems.at[i]))
        copies[-1].start()
    for copy in copies:
        copy.wait()


def columns_of(at, w, part, count, width):
    return pl.pallas_call(
        functools.partial(columns_kernel, part * count),
        out_shape=pltpu.VMEM((count, w.shape[0], width), w.dtype),
        in_specs=[pl.BlockSpec(memory_space=pltpu.SMEM), pl.BlockSpec(memory_space=pltpu.HBM)],
        out_specs=pl.BlockSpec(memory_space=pltpu.VMEM),
        scratch_shapes=[pltpu.SemaphoreType.DMA((count,))],
        compiler_params=pltpu.CompilerParams(vmem_limit_bytes=8 << 20),
    )(at, pltpu.with_memory_space_constraint(w, pltpu.HBM))


def spread_own_kernel(at_ref, own_ref, w_ref, out_ref):
    out_ref[0] = jnp.dot(own_ref[...], w_ref[...], preferred_element_type=jnp.float32)


def spread_own(at, own, w, width):
    rows, depth = own.shape
    count = len(SHIFTS)
    return pl.pallas_call(
        spread_own_kernel,
        out_shape=pltpu.VMEM((count, rows, width), jnp.float32),
        grid_spec=pltpu.PrefetchScalarGridSpec(
            num_scalar_prefetch=1,
            grid=(count,),
            in_specs=[
                pl.BlockSpec((rows, depth), lambda i, at: (0, 0)),
                pl.BlockSpec((depth, width), lambda i, at: (0, at[HERE_AT + i])),
            ],
            out_specs=pl.BlockSpec((1, rows, width), lambda i, at: (i, 0, 0)),
        ),
        compiler_params=pltpu.CompilerParams(vmem_limit_bytes=8 << 20),
        name="spread_own",
    )(at, own, pltpu.with_memory_space_constraint(w, pltpu.HBM))


def spread_kernel(lo, index_ref, other_ref, a_ref, b_ref, c_ref, d_ref, base_ref, out_ref, held):
    @pl.loop(0, out_ref.shape[0])
    def _(i):
        place, side = index_ref[PLACE_AT + lo + i], index_ref[SIDE_AT + lo + i]
        source = side * 2 + place // 2

        for at, ref in enumerate((a_ref, b_ref, c_ref, d_ref)):

            @pl.when(source == at)
            def _():
                held[...] = ref[place % 2]

        out_ref[i] = base_ref[lo + i] + jnp.dot(
            other_ref[...], held[...], preferred_element_type=jnp.float32
        )


def toeplitz_kernel(mr_ref, out_ref, taps_ref):
    shape = (TAPS_MR, 2 * TAPS_MR)
    from_tap = lax.broadcasted_iota(jnp.int32, shape, 0)
    to_lane = lax.broadcasted_iota(jnp.int32, shape, 1)
    flip = jnp.where(from_tap + to_lane == TAPS_MR, 1.0, 0.0).astype(jnp.bfloat16)
    taps_ref[...] = jnp.dot(mr_ref[...], flip, preferred_element_type=jnp.float32)

    @pl.loop(0, out_ref.shape[0])
    def _(group):
        row = jnp.broadcast_to(taps_ref[pl.ds(group, 1), :], shape)
        out_ref[group] = pltpu.roll(row, 0, 1, stride=1, stride_axis=0).astype(jnp.bfloat16)


def toeplitz_of(filters):
    groups = filters.shape[0]
    out = ((groups, TAPS_MR, 2 * TAPS_MR), jnp.bfloat16)
    scratch = [pltpu.VMEM((groups, 2 * TAPS_MR), jnp.float32)]
    return kernel_of(toeplitz_kernel, out, scratch=scratch)(filters)


def filter_kernel(
    qp_ref, kp_ref, vp_ref, qr_ref, kvr_ref, taps_ref, toep_ref, out_ref, k_ref, v_ref, q_ref, g_ref
):
    rows, slab = out_ref.shape
    lane = lax.broadcasted_iota(jnp.int32, (2 * TAPS_MR, TILE), 1) // GROUP

    def filtered(ref, first, count, stream, start):
        total = None
        for by in range(TAPS_SHORT):
            tap = taps_ref[stream, pl.ds(by, 1), pl.ds(start, TILE)]
            term = tap * ref[pl.ds(first - by, count), :]
            total = term if total is None else total + term
        return total

    @pl.loop(0, slab // TILE)
    def _(tile):
        start = pl.multiple_of(tile * TILE, TILE)
        cols = pl.ds(start, TILE)
        k_ref[pl.ds(0, RIM), :] = kvr_ref[0, :, cols].astype(jnp.float32)
        v_ref[pl.ds(0, RIM), :] = kvr_ref[1, :, cols].astype(jnp.float32)
        q_ref[pl.ds(0, 8), :] = qr_ref[:, cols].astype(jnp.float32)[8:]
        k_ref[pl.ds(RIM, rows), :] = kp_ref[:, cols]
        v_ref[pl.ds(RIM, rows), :] = vp_ref[:, cols]
        q_ref[pl.ds(8, rows), :] = qp_ref[:, cols]
        for block in range((rows + TAPS_MR) // TAPS_MR):
            first = block * TAPS_MR + RIM - TAPS_MR
            gate = filtered(k_ref, first, TAPS_MR, 1, start) * filtered(v_ref, first, TAPS_MR, 2, start)
            g_ref[pl.ds(block * TAPS_MR, TAPS_MR), :] = gate.astype(jnp.bfloat16)
        for block in range(rows // TAPS_MR):
            window = g_ref[pl.ds(block * TAPS_MR, 2 * TAPS_MR), :]
            total = None
            for group in range(TILE // GROUP):
                picked = jnp.where(lane == group, window, jnp.zeros_like(window))
                term = jnp.dot(
                    toep_ref[tile * (TILE // GROUP) + group], picked, preferred_element_type=jnp.float32
                )
                total = term if total is None else total + term
            query = filtered(q_ref, 8 + block * TAPS_MR, TAPS_MR, 0, start)
            out_ref[pl.ds(block * TAPS_MR, TAPS_MR), pl.ds(start, TILE)] = (query * total).astype(jnp.bfloat16)


def filtering(q, k, v, q_rim, kv_rim, taps, toeplitz):
    rows, slab = q.shape
    scratch = [
        pltpu.VMEM((RIM + rows, TILE), jnp.float32),
        pltpu.VMEM((RIM + rows, TILE), jnp.float32),
        pltpu.VMEM((8 + rows, TILE), jnp.float32),
        pltpu.VMEM((TAPS_MR + rows, TILE), jnp.bfloat16),
    ]
    call = kernel_of(filter_kernel, ((rows, slab), jnp.bfloat16), scratch=scratch, limit=10)
    return call(q, k, v, q_rim, kv_rim, taps, toeplitz)


def local(hidden, w_feature, short_filter, mr_filter, w_out):
    rows, feats = hidden.shape
    slab = w_feature.shape[2]
    width = w_out.shape[1] // (2 * NZ)
    device = lax.axis_index("ctx") * 16 + lax.axis_index("tp")
    table = lax.dynamic_slice_in_dim(jnp.asarray(tables()), device, 1, 0)[0]

    toeplitz = toeplitz_of(mr_filter)
    mine = send(hidden, swapped)
    mine, table = lax.optimization_barrier((mine, table))

    w_own = w_feature.transpose(1, 0, 2)
    after = send(w_own, along_x(-1))
    before = send(w_own, along_x(1))
    far_lo = send(after[:, : feats // 2], along_x(-1))
    far_hi = send(before[:, feats // 2 :], along_x(1))
    far = kernel_of(join_kernel, ((3, feats, slab), jnp.bfloat16))(far_lo, far_hi)
    weights = (w_own, after, far, before)

    w_near = [send(columns_of(table, w_out, h, 2, width), other_yl) for h in (0, 1)]
    w_far = [send(w_near[h], other_core) for h in (0, 1)]
    own = [mine, send(mine, other_yl)]
    t1, o1, t2, o2, t3, o3 = [], [], [], [], [], []
    for e in (0, 1):
        t1.append(send(own[e], to_partner))
        o1.append(send(own[e], to_other))
        t2.append(send(o1[e], to_partner))
        o2.append(send(t1[e], to_other))
        t3.append(send(o2[e], to_partner))
        o3.append(send(t2[e], to_other))
    last = [send(o3[0], to_partner)]
    last.append(send(last[0], other_yl))

    blocks = [b for pair in (own, t1, o2, o1, t2, t3, last, o3) for b in pair]
    held = kernel_of(arrange_kernel, ((16, rows, feats), jnp.bfloat16), 1)(table, *blocks)

    def stream_of(p):
        out = ((4, rows, slab), jnp.bfloat16)
        call = kernel_of(product_kernel, out, 1, limit=14)
        partial = call(jnp.full((1,), p, jnp.int32), held, *weights)
        got = send(partial[2:], other_core)
        pair = partial[:2].astype(jnp.float32) + got.astype(jnp.float32)
        rest = send(pair[1].astype(jnp.bfloat16), other_yh).astype(jnp.float32)
        return pair[0] + rest

    k, v, q = stream_of(1), stream_of(2), stream_of(0)
    kv_rim = jnp.stack([k[rows - RIM :], v[rows - RIM :]]).astype(jnp.bfloat16)
    kv_rim = send(kv_rim, next_block)
    q_rim = send(q[rows - 16 :].astype(jnp.bfloat16), next_block)
    mixer = filtering(q, k, v, q_rim, kv_rim, short_filter.transpose(1, 0, 2), toeplitz)
    mixer_other = send(mixer, other_yl)

    base = spread_own(table, mixer, w_out, width)

    def spread(lo, count):
        call = kernel_of(
            functools.partial(spread_kernel, lo),
            ((count, rows, width), jnp.float32),
            1,
            [pltpu.VMEM((feats, width), jnp.bfloat16)],
            limit=14,
        )
        return call(table, mixer_other, *w_near, *w_far, base)

    early = spread(0, 3)
    late = spread(3, 5)
    part = {by: early[i] if i < 3 else late[i - 3] for i, by in enumerate(SHIFTS)}
    half = width // 2
    cols = [slice(0, half), slice(half, width)]
    ups = [part[4][:, cols[0]].astype(jnp.bfloat16), None]
    downs = [None, part[4][:, cols[1]].astype(jnp.bfloat16)]
    for step in range(1, 5):
        ups = [None if u is None else send(u, along_z(1)) for u in ups]
        downs = [None if d is None else send(d, along_z(-1)) for d in downs]
        if step == 4:
            break
        for h in (0, 1):
            up, down = part[4 - step][:, cols[h]], part[step - 4][:, cols[h]]
            if ups[h] is not None:
                up = up + ups[h].astype(jnp.float32)
            if downs[h] is not None:
                down = down + downs[h].astype(jnp.float32)
            ups[h], downs[h] = up.astype(jnp.bfloat16), down.astype(jnp.bfloat16)
    sums = [
        part[0][:, cols[h]] + ups[h].astype(jnp.float32) + downs[h].astype(jnp.float32) for h in (0, 1)
    ]
    return jnp.concatenate(sums, 1).astype(jnp.bfloat16)


def solution(mesh):
    return jax.shard_map(
        local,
        mesh=mesh,
        in_specs=(
            P("ctx", "tp"),
            P("ctx", None, "tp"),
            P(None, None, "tp"),
            P("tp", None),
            P("tp", None),
        ),
        out_specs=P("ctx", "tp"),
        check_vma=False,
    )
```

```python
import functools

import jax
import jax.numpy as jnp
import numpy as np
from jax import lax
from jax.experimental import pallas as pl
from jax.experimental.pallas import tpu as pltpu
from jax.sharding import PartitionSpec as P

TAPS_SHORT = 7
TAPS_MR = 128
GROUP = 16
NX, NZ = 4, 8
RIM = 136
TILE = 256


def pairs_of(move):
    out = []
    for x in range(NX):
        for yh in range(2):
            for core in range(2):
                for z in range(NZ):
                    for yl in range(2):
                        to = move(x, yh, core, z, yl)
                        if to is None:
                            continue
                        tx, tyh, tcore, tz, tyl = to
                        here = ((x * 2 + yh) * 2 + core) * 16 + z * 2 + yl
                        there = ((tx * 2 + tyh) * 2 + tcore) * 16 + tz * 2 + tyl
                        out.append((here, there))
    return out


SHIFTS = (4, 3, -3, 2, -2, 1, -1, 0)
ORDER_AT, HERE_AT, SIDE_AT, PLACE_AT, AWAY_AT, COUNT = 0, 16, 24, 32, 40, 128


def tables():
    rows = np.zeros((256, COUNT), np.int32)
    for device in range(256):
        ctx, tp = divmod(device, 16)
        x, yh, core, z, yl = ctx // 4, (ctx // 2) % 2, ctx % 2, tp // 2, tp % 2
        row = []
        for even in (0, -1, 1, 2):
            by = even * (1 - 2 * (z % 2))
            for differs in (0, 1):
                for e in (0, 1):
                    token = (yl ^ e ^ core) * 2 + ((z % 2) ^ differs ^ yh)
                    row.append(((z // 2 + by - x) % NX) * 4 + token)
        to = [(z + by) % NZ for by in SHIFTS]
        row += [t * 2 + yl for t in to] + [(t // 4) ^ core for t in to] + [t % 4 for t in to]
        row += [(core * 4 + t) * 2 + 1 - yl for t in range(4)]
        rows[device, : len(row)] = row
    return rows


def send(value, move):
    return lax.ppermute(value, ("ctx", "tp"), pairs_of(move))


def along_x(by):
    return lambda x, yh, core, z, yl: ((x + by) % NX, yh, core, z, yl)


def along_z(by):
    return lambda x, yh, core, z, yl: (x, yh, core, (z + by) % NZ, yl)


def other_yh(x, yh, core, z, yl):
    return x, 1 - yh, core, z, yl


def other_core(x, yh, core, z, yl):
    return x, yh, 1 - core, z, yl


def other_yl(x, yh, core, z, yl):
    return x, yh, core, z, 1 - yl


def swapped(x, yh, core, z, yl):
    return x, z % 2, yl, z - z % 2 + yh, core


def to_partner(x, yh, core, z, yl):
    return x, yh, core, z ^ 1, yl


def to_other(x, yh, core, z, yl):
    return x, yh, core, (z + (1 if z % 2 else -1)) % NZ, yl


def next_block(x, yh, core, z, yl):
    block = (x * 2 + yh) * 2 + core + 1
    if block == 16:
        return None
    return block // 4, (block // 2) % 2, block % 2, z, yl


def in_vmem(value):
    return pltpu.with_memory_space_constraint(value, pltpu.VMEM)


def kernel_of(body, out, scalars=0, scratch=(), limit=8):
    whole = pl.BlockSpec(memory_space=pltpu.VMEM)

    def call(*args):
        placed = [*args[:scalars], *(in_vmem(a) for a in args[scalars:])]
        return pl.pallas_call(
            body,
            out_shape=pltpu.VMEM(*out),
            in_specs=[pl.BlockSpec(memory_space=pltpu.SMEM)] * scalars + [whole] * (len(args) - scalars),
            out_specs=whole,
            scratch_shapes=list(scratch),
            compiler_params=pltpu.CompilerParams(vmem_limit_bytes=limit << 20),
        )(*placed)

    return call


def join_kernel(lo_ref, hi_ref, out_ref):
    half = lo_ref.shape[1]
    out_ref[:, :half, :] = lo_ref[...]
    out_ref[:, half:, :] = hi_ref[...]


def arrange_kernel(order_ref, *refs):
    out_ref = refs[-1]
    for slot, ref in enumerate(refs[:-1]):
        out_ref[order_ref[ORDER_AT + slot]] = ref[...]


def product_kernel(stream_ref, held_ref, *refs):
    out_ref = refs[-1]
    stream = stream_ref[0]

    @pl.loop(0, 4)
    def _(token):
        total = None
        for part, ref in enumerate(refs[:-1]):
            term = jnp.dot(held_ref[part * 4 + token], ref[stream], preferred_element_type=jnp.float32)
            total = term if total is None else total + term
        out_ref[token] = total.astype(jnp.bfloat16)


def columns_kernel(first, at_ref, w_ref, out_ref, sems):
    width = out_ref.shape[2]
    copies = []
    for i in range(out_ref.shape[0]):
        cols = pl.ds(pl.multiple_of(at_ref[AWAY_AT + first + i] * width, width), width)
        copies.append(pltpu.make_async_copy(w_ref.at[:, cols], out_ref.at[i], sems.at[i]))
        copies[-1].start()
    for copy in copies:
        copy.wait()


def columns_of(at, w, first, count, width):
    return pl.pallas_call(
        functools.partial(columns_kernel, first),
        out_shape=pltpu.VMEM((count, w.shape[0], width), w.dtype),
        in_specs=[pl.BlockSpec(memory_space=pltpu.SMEM), pl.BlockSpec(memory_space=pltpu.HBM)],
        out_specs=pl.BlockSpec(memory_space=pltpu.VMEM),
        scratch_shapes=[pltpu.SemaphoreType.DMA((count,))],
        compiler_params=pltpu.CompilerParams(vmem_limit_bytes=8 << 20),
    )(at, pltpu.with_memory_space_constraint(w, pltpu.HBM))


def spread_own_kernel(at_ref, own_ref, w_ref, out_ref):
    out_ref[0] = jnp.dot(own_ref[...], w_ref[...], preferred_element_type=jnp.float32)


def spread_own(at, own, w, width):
    rows, depth = own.shape
    count = len(SHIFTS)
    return pl.pallas_call(
        spread_own_kernel,
        out_shape=pltpu.VMEM((count, rows, width), jnp.float32),
        grid_spec=pltpu.PrefetchScalarGridSpec(
            num_scalar_prefetch=1,
            grid=(count,),
            in_specs=[
                pl.BlockSpec((rows, depth), lambda i, at: (0, 0)),
                pl.BlockSpec((depth, width), lambda i, at: (0, at[HERE_AT + i])),
            ],
            out_specs=pl.BlockSpec((1, rows, width), lambda i, at: (i, 0, 0)),
        ),
        compiler_params=pltpu.CompilerParams(vmem_limit_bytes=8 << 20),
        name="spread_own",
    )(at, own, pltpu.with_memory_space_constraint(w, pltpu.HBM))


def spread_kernel(lo, index_ref, other_ref, a_ref, b_ref, c_ref, d_ref, base_ref, out_ref, held):
    @pl.loop(0, out_ref.shape[0])
    def _(i):
        place, side = index_ref[PLACE_AT + lo + i], index_ref[SIDE_AT + lo + i]
        source = side * 2 + place // 3

        for at, ref in enumerate((a_ref, b_ref, c_ref, d_ref)):

            @pl.when(source == at)
            def _():
                held[...] = ref[place % 3]

        out_ref[i] = base_ref[lo + i] + jnp.dot(
            other_ref[...], held[...], preferred_element_type=jnp.float32
        )


def toeplitz_kernel(mr_ref, out_ref, taps_ref):
    shape = (TAPS_MR, 2 * TAPS_MR)
    from_tap = lax.broadcasted_iota(jnp.int32, shape, 0)
    to_lane = lax.broadcasted_iota(jnp.int32, shape, 1)
    flip = jnp.where(from_tap + to_lane == TAPS_MR, 1.0, 0.0).astype(jnp.bfloat16)
    taps_ref[...] = jnp.dot(mr_ref[...], flip, preferred_element_type=jnp.float32)

    @pl.loop(0, out_ref.shape[0])
    def _(group):
        row = jnp.broadcast_to(taps_ref[pl.ds(group, 1), :], shape)
        out_ref[group] = pltpu.roll(row, 0, 1, stride=1, stride_axis=0).astype(jnp.bfloat16)


def toeplitz_of(filters):
    groups = filters.shape[0]
    out = ((groups, TAPS_MR, 2 * TAPS_MR), jnp.bfloat16)
    scratch = [pltpu.VMEM((groups, 2 * TAPS_MR), jnp.float32)]
    return kernel_of(toeplitz_kernel, out, scratch=scratch)(filters)


def filtered(ref, taps_ref, first, stream, start):
    total = None
    for by in range(TAPS_SHORT):
        tap = taps_ref[stream, pl.ds(by, 1), pl.ds(start, TILE)]
        term = tap * ref[pl.ds(first - by, TAPS_MR), :]
        total = term if total is None else total + term
    return total


def conv_kernel(kp_ref, vp_ref, rim_ref, taps_ref, toep_ref, out_ref, k_ref, v_ref, g_ref):
    rows, slab = out_ref.shape
    lane = lax.broadcasted_iota(jnp.int32, (2 * TAPS_MR, TILE), 1) // GROUP

    @pl.loop(0, slab // TILE)
    def _(tile):
        start = pl.multiple_of(tile * TILE, TILE)
        cols = pl.ds(start, TILE)
        k_ref[pl.ds(0, RIM), :] = rim_ref[0, :, cols].astype(jnp.float32)
        v_ref[pl.ds(0, RIM), :] = rim_ref[1, :, cols].astype(jnp.float32)
        k_ref[pl.ds(RIM, rows), :] = kp_ref[:, cols]
        v_ref[pl.ds(RIM, rows), :] = vp_ref[:, cols]
        for block in range((rows + TAPS_MR) // TAPS_MR):
            first = block * TAPS_MR + RIM - TAPS_MR
            gate = filtered(k_ref, taps_ref, first, 1, start) * filtered(v_ref, taps_ref, first, 2, start)
            g_ref[pl.ds(block * TAPS_MR, TAPS_MR), :] = gate.astype(jnp.bfloat16)
        for block in range(rows // TAPS_MR):
            window = g_ref[pl.ds(block * TAPS_MR, 2 * TAPS_MR), :]
            total = None
            for group in range(TILE // GROUP):
                picked = jnp.where(lane == group, window, jnp.zeros_like(window))
                toep = toep_ref[tile * (TILE // GROUP) + group]
                term = jnp.dot(toep, picked, preferred_element_type=jnp.float32)
                total = term if total is None else total + term
            out_ref[pl.ds(block * TAPS_MR, TAPS_MR), cols] = total


def gate_kernel(qp_ref, rim_ref, taps_ref, long_ref, out_ref, q_ref):
    rows, slab = out_ref.shape

    @pl.loop(0, slab // TILE)
    def _(tile):
        start = pl.multiple_of(tile * TILE, TILE)
        cols = pl.ds(start, TILE)
        q_ref[pl.ds(0, 8), :] = rim_ref[:, cols].astype(jnp.float32)[8:]
        q_ref[pl.ds(8, rows), :] = qp_ref[:, cols]
        for block in range(rows // TAPS_MR):
            at = pl.ds(block * TAPS_MR, TAPS_MR)
            query = filtered(q_ref, taps_ref, 8 + block * TAPS_MR, 0, start)
            out_ref[at, cols] = (query * long_ref[at, cols]).astype(jnp.bfloat16)


def filtering(q, k, v, q_rim, kv_rim, taps, toeplitz):
    rows, slab = q.shape
    scratch = [
        pltpu.VMEM((RIM + rows, TILE), jnp.float32),
        pltpu.VMEM((RIM + rows, TILE), jnp.float32),
        pltpu.VMEM((TAPS_MR + rows, TILE), jnp.bfloat16),
    ]
    conv = kernel_of(conv_kernel, ((rows, slab), jnp.float32), scratch=scratch, limit=10)
    long_out = conv(k, v, kv_rim, taps, toeplitz)
    scratch = [pltpu.VMEM((8 + rows, TILE), jnp.float32)]
    gate = kernel_of(gate_kernel, ((rows, slab), jnp.bfloat16), scratch=scratch)
    return gate(q, q_rim, taps, long_out)


def local(hidden, w_feature, short_filter, mr_filter, w_out):
    rows, feats = hidden.shape
    slab = w_feature.shape[2]
    width = w_out.shape[1] // (2 * NZ)
    device = lax.axis_index("ctx") * 16 + lax.axis_index("tp")
    table = lax.dynamic_slice_in_dim(jnp.asarray(tables()), device, 1, 0)[0]

    toeplitz = toeplitz_of(mr_filter)
    mine = send(hidden, swapped)
    mine, table = lax.optimization_barrier((mine, table))

    w_own = w_feature.transpose(1, 0, 2)
    after = send(w_own, along_x(-1))
    before = send(w_own, along_x(1))
    far_lo = send(after[:, : feats // 2], along_x(-1))
    far_hi = send(before[:, feats // 2 :], along_x(1))
    far = kernel_of(join_kernel, ((3, feats, slab), jnp.bfloat16))(far_lo, far_hi)
    weights = (w_own, after, far, before)

    w_near = [send(columns_of(table, w_out, first, count, width), other_yl) for first, count in ((0, 3), (3, 1))]
    w_far = [send(w_near[h], other_core) for h in (0, 1)]
    own = [mine, send(mine, other_yl)]
    t1, o1, t2, o2, t3, o3 = [], [], [], [], [], []
    for e in (0, 1):
        t1.append(send(own[e], to_partner))
        o1.append(send(own[e], to_other))
        t2.append(send(o1[e], to_partner))
        o2.append(send(t1[e], to_other))
        t3.append(send(o2[e], to_partner))
        o3.append(send(t2[e], to_other))
    last = [send(o3[0], to_partner)]
    last.append(send(last[0], other_yl))

    blocks = [b for pair in (own, t1, o2, o1, t2, t3, last, o3) for b in pair]
    held = kernel_of(arrange_kernel, ((16, rows, feats), jnp.bfloat16), 1)(table, *blocks)

    def stream_of(p):
        out = ((4, rows, slab), jnp.bfloat16)
        call = kernel_of(product_kernel, out, 1, limit=14)
        partial = call(jnp.full((1,), p, jnp.int32), held, *weights)
        got = send(partial[2:], other_core)
        pair = partial[:2].astype(jnp.float32) + got.astype(jnp.float32)
        rest = send(pair[1].astype(jnp.bfloat16), other_yh).astype(jnp.float32)
        return pair[0] + rest

    k, v, q = stream_of(1), stream_of(2), stream_of(0)
    kv_rim = jnp.stack([k[rows - RIM :], v[rows - RIM :]]).astype(jnp.bfloat16)
    kv_rim = send(kv_rim, next_block)
    q_rim = send(q[rows - 16 :].astype(jnp.bfloat16), next_block)
    mixer = filtering(q, k, v, q_rim, kv_rim, short_filter.transpose(1, 0, 2), toeplitz)
    mixer_other = send(mixer, other_yl)

    base = spread_own(table, mixer, w_out, width)

    def spread(lo, count):
        call = kernel_of(
            functools.partial(spread_kernel, lo),
            ((count, rows, width), jnp.float32),
            1,
            [pltpu.VMEM((feats, width), jnp.bfloat16)],
            limit=14,
        )
        return call(table, mixer_other, *w_near, *w_far, base)

    early = spread(0, 3)
    late = spread(3, 5)
    part = {by: early[i] if i < 3 else late[i - 3] for i, by in enumerate(SHIFTS)}
    half = width // 2
    cols = [slice(0, half), slice(half, width)]
    ups = [part[4][:, cols[0]].astype(jnp.bfloat16), None]
    downs = [None, part[4][:, cols[1]].astype(jnp.bfloat16)]
    for step in range(1, 5):
        ups = [None if u is None else send(u, along_z(1)) for u in ups]
        downs = [None if d is None else send(d, along_z(-1)) for d in downs]
        if step == 4:
            break
        for h in (0, 1):
            up, down = part[4 - step][:, cols[h]], part[step - 4][:, cols[h]]
            if ups[h] is not None:
                up = up + ups[h].astype(jnp.float32)
            if downs[h] is not None:
                down = down + downs[h].astype(jnp.float32)
            ups[h], downs[h] = up.astype(jnp.bfloat16), down.astype(jnp.bfloat16)
    sums = [
        part[0][:, cols[h]] + ups[h].astype(jnp.float32) + downs[h].astype(jnp.float32) for h in (0, 1)
    ]
    return jnp.concatenate(sums, 1).astype(jnp.bfloat16)


def solution(mesh):
    return jax.shard_map(
        local,
        mesh=mesh,
        in_specs=(
            P("ctx", "tp"),
            P("ctx", None, "tp"),
            P(None, None, "tp"),
            P("tp", None),
            P("tp", None),
        ),
        out_specs=P("ctx", "tp"),
        check_vma=False,
    )
```
